256 devices in a mesh: seq: 32 (over y, z_hi, x), grp: 8 (over z_lo, core).
Axes of the slice: x: 4, y: 4, z: 8 (z_hi: 2, z_lo: 4; z = z_hi * 4 + z_lo), core: 2. Of those that a mesh axis runs over, the one named last changes fastest.
Arguments:
- inputs: bfloat16 [4096, 8192], P('seq', 'grp'), may hold values from -10 to 10
- query_states: bfloat16 [4096, 8192], P('seq', 'grp'), may hold values from -12 to 12
- key_states: bfloat16 [4096, 1024], P('seq', 'grp'), may hold values from -6 to 6
- value_states: bfloat16 [4096, 1024], P('seq', 'grp'), may hold values from -6 to 6
- doc_ids: int32 [4096], replicated, may hold values from 0 to 7, never falling along the last dimension, each value on 1 to 3072 neighbouring positions
- modality: int32 [4096], P('seq'), may hold values from 0 to 1, as said below
- expert_ids: int32 [4096, 4], P('seq'), may hold values from -1 to 31, as said below
- norm_gain: float32 [8192], P('grp'), may hold values from 0.1 to 1.9
- router_w: bfloat16 [8192, 64], P('grp'), may hold values from -0.0625 to 0.0625
- w_in: bfloat16 [2, 32, 8192, 1408], P(None, 'seq', 'grp'), may hold values from -1 to 1
- w_out: bfloat16 [2, 32, 1408, 8192], P(None, 'seq', None, 'grp'), may hold values from -2 to 2
- grad_out: bfloat16 [4096, 8192], P('seq', 'grp'), may hold values from -12 to 12
Outputs:
- layer_out: bfloat16 [4096, 8192], P('seq', 'grp')
- state_grad: bfloat16 [4096, 8192], P('seq', 'grp')
The draws below stay inside these ranges and needn't reach their ends.
Inputs may be any that keep to these rules, and one draw needn't show every extreme that they name: Modality is constant over aligned runs of 16 tokens; every block of 128 tokens held by one index of seq has a run of each modality. `expert_ids`: -1 marks an empty choice; the other entries of a token are distinct experts of its modality. At most 16 choices of the 128 tokens of one index of seq name one expert of one modality, and in every draw one text expert and one image expert are named by exactly 16 choices of every such block.
All inputs are finite; a program needn't handle non-finite values.
Results may differ from the reference program's by a relative error of at most 0.008.
Values may be sent and summed in bfloat16 or wider, within the bound.
A program may use at most 128 MiB of HBM per device.

```python
import math
import jax
import jax.numpy as jnp
import numpy as np
from jax import lax

D = 8192
HEADS = 64
KV_HEADS = 8
HEAD_DIM = 128
FF = 1408
TOP = 4
DOCS = 8
LEN_DEV = 128
CAP = 16
EXPERTS = 32
TOKENS = 4096
N_SEQ = 32
N_GRP = 8


def route_plan(key):
    base_key = jax.random.fold_in(key, 17)
    k_kind, k_order, k_hot, k_score, k_empty = jax.random.split(base_key, 5)
    blocks = TOKENS // LEN_DEV
    run_count = LEN_DEV // CAP
    run_kinds = jax.random.randint(k_kind, (blocks, run_count), 0, 2)
    orders = jax.vmap(lambda one_key: jax.random.permutation(one_key, run_count))(jax.random.split(k_order, blocks))
    first_run = orders[:, 0]
    second = orders[:, 1]
    run_index = jnp.arange(run_count)[None, :]
    run_kinds = jnp.where(run_index == first_run[:, None], 0, run_kinds)
    run_kinds = jnp.where(run_index == second[:, None], 1, run_kinds)
    forced = (run_index == first_run[:, None]) | (run_index == second[:, None])
    modality = jnp.repeat(run_kinds, CAP, axis=1).reshape(TOKENS).astype(jnp.int32)
    forced_tok = jnp.repeat(forced, CAP, axis=1).reshape(TOKENS)
    hot_expert = jax.random.randint(k_hot, (2,), 0, EXPERTS)
    hot_tok = hot_expert[modality]
    expert_range = jnp.arange(EXPERTS, dtype=jnp.int32)[None, :]
    scores = jax.random.randint(k_score, (TOKENS, EXPERTS), 0, 1 << 20) * EXPERTS + expert_range
    boosted = scores + (forced_tok[:, None] & (expert_range == hot_tok[:, None])).astype(jnp.int32) * (1 << 28)
    choice_ids = lax.top_k(boosted, TOP)[1].astype(jnp.int32)
    empty_slot = (jax.random.randint(k_empty, (TOKENS, TOP), 0, 4) == 0) & (jnp.arange(TOP)[None, :] > 0)
    choice_ids = jnp.where(empty_slot, -1, choice_ids)
    column = modality[:, None] * EXPERTS + jnp.maximum(choice_ids, 0)
    one_hot = ((column[:, :, None] == jnp.arange(2 * EXPERTS)[None, None, :]) & (choice_ids[:, :, None] >= 0)).astype(jnp.int32)
    one_hot = one_hot.reshape(blocks, LEN_DEV * TOP, 2 * EXPERTS)
    earlier_count = jnp.cumsum(one_hot, axis=1) - one_hot
    slot_rank = jnp.sum(earlier_count * one_hot, axis=2).reshape(TOKENS, TOP)
    choice_ids = jnp.where(slot_rank >= CAP, -1, choice_ids)
    return (modality, choice_ids.astype(jnp.int32))


def draw_modality(key, part):
    return route_plan(key)[0]


def draw_expert_ids(key, part):
    return route_plan(key)[1]


def draw_query_states(key, part):
    own_key = jax.random.fold_in(key, 31)
    result = jnp.clip(jax.random.normal(own_key, (TOKENS, HEADS * HEAD_DIM)), -6.0, 6.0)
    return result.astype(jnp.float32).astype(jnp.bfloat16)


def draw_key_states(key, part):
    own_key = jax.random.fold_in(key, 37)
    result = jnp.clip(jax.random.normal(own_key, (TOKENS, KV_HEADS * HEAD_DIM)), -6.0, 6.0)
    return result.astype(jnp.float32).astype(jnp.bfloat16)


def feature_scale(key):
    order = jax.random.permutation(jax.random.fold_in(key, 47), 8)
    level = 0.25 * 10.0 ** (order.astype(jnp.float32) / 7.0)
    group = jnp.arange(D, dtype=jnp.int32) // (D // 8)
    return jnp.sqrt(level[group])


def drawn_stream(key):
    stream_key = jax.random.fold_in(key, 43)
    values = jnp.clip(jax.random.normal(stream_key, (TOKENS, D)), -6.0, 6.0)
    return values * feature_scale(key)[None, :]


def draw_inputs(key, part):
    result = drawn_stream(key)
    return result.astype(jnp.float32).astype(jnp.bfloat16)


def draw_grad_out(key, part):
    noise_key = jax.random.fold_in(key, 59)
    base_vals = drawn_stream(key)
    noise = jnp.clip(jax.random.normal(noise_key, (TOKENS, D)), -6.0, 6.0)
    return (0.9 * base_vals + 0.4 * noise).astype(jnp.float32).astype(jnp.bfloat16)


def unit_normal(sample_key, shape):
    return jnp.clip(jax.random.normal(sample_key, shape), -6.0, 6.0)


def expert_key(key, expert_index):
    return jax.random.fold_in(jax.random.fold_in(key, 53), expert_index)


def draw_w_in(key, part):
    sampler = unit_normal

    def one_expert(expert_index):
        base_vals = sampler(jax.random.fold_in(expert_key(key, expert_index), 1), (D, FF))
        return (base_vals * D ** (-0.5)).astype(jnp.float32).astype(jnp.bfloat16)
    stacked = lax.map(one_expert, jnp.arange(2 * EXPERTS, dtype=jnp.int32))
    return stacked.reshape(2, EXPERTS, D, FF)


def draw_w_out(key, part):
    sampler = unit_normal

    def one_expert(expert_index):
        own_key = expert_key(key, expert_index)
        base_vals = sampler(jax.random.fold_in(own_key, 1), (D, FF))
        noise = sampler(jax.random.fold_in(own_key, 2), (FF, D))
        mixed = (0.9 * base_vals.T + 0.4359 * noise) * FF ** (-0.5)
        return mixed.astype(jnp.float32).astype(jnp.bfloat16)
    stacked = lax.map(one_expert, jnp.arange(2 * EXPERTS, dtype=jnp.int32))
    return stacked.reshape(2, EXPERTS, FF, D)


def block_levels(key, dims, cuts, least, largest):
    gain, own = 1.0, jax.random.fold_in(key, 6)
    for dim, blocks in cuts:
        heights = jnp.exp(jax.random.uniform(jax.random.fold_in(own, dim), (blocks,), jnp.float32, least / len(cuts), largest / len(cuts)))
        gain = gain * jnp.repeat(heights, dims[dim] // blocks).reshape([-1 if axis == dim else 1 for axis in range(len(dims))])
    return gain


def split_up(amount, total, reach, lean):
    weights = [(1 << 20) // math.isqrt(standing ** lean) + 1 for standing in range(2, amount + 1)]
    rest, holding = total - reach - (amount - 1), [1] * (amount - 1)
    while rest > 0:
        candidates = [i for i in range(amount - 1) if holding[i] < reach]
        whole, left = sum([weights[i] for i in candidates]), rest
        for i in candidates:
            extra = min(reach - holding[i], max(1, left * weights[i] // whole), rest)
            holding[i] = holding[i] + extra
            rest = rest - extra
    return np.array([reach] + holding)


def ragged(key, number_of, total, limit, lean):
    if number_of == 2:
        one = jax.random.randint(key, (), max(1, total - limit), min(limit, total - 1) + 1)
        return jnp.stack([one, total - one])
    sizes = jnp.asarray(split_up(number_of, total, limit, lean), jnp.int32)
    pairs = (number_of - 1) // 2
    giver, receiver = sizes[1:1 + 2 * pairs:2], sizes[2:2 + 2 * pairs:2]
    margin = jnp.minimum(giver - 1, limit - receiver)
    moved = jax.random.randint(jax.random.fold_in(key, 1), (pairs,), 0, 1 << 20) % (margin + 1)
    sizes = sizes.at[1:1 + 2 * pairs:2].set(giver - moved).at[2:2 + 2 * pairs:2].set(receiver + moved)
    return sizes[jax.random.permutation(jax.random.fold_in(key, 2), number_of)]


def gaussian(rng, dims, deviation, reach, cuts=(), kind=jnp.bfloat16):
    entries = deviation * jax.random.normal(rng, dims, jnp.float32)
    if cuts:
        entries = entries * block_levels(rng, dims, cuts, -0.22, 0.18)
    return jnp.clip(entries, -reach, reach).astype(kind)


def setup_inputs(seed: int = 0) -> dict:
    seeds = jax.random.split(jax.random.key(seed), 13)
    inputs = draw_inputs(jax.random.fold_in(seeds[12], 71), 0)
    query_states = draw_query_states(jax.random.fold_in(seeds[12], 71), 0)
    key_states = draw_key_states(jax.random.fold_in(seeds[12], 71), 0)
    value_states = gaussian(seeds[3], (TOKENS, KV_HEADS * HEAD_DIM), 1.0, 6.0, ((0, 32), (1, 8)))
    doc_ids = jnp.searchsorted(jnp.cumsum(ragged(seeds[4], DOCS, TOKENS, 3 * TOKENS // 4, 2)), jnp.arange(TOKENS), side="right").astype(jnp.int32)
    modality = draw_modality(jax.random.fold_in(seeds[12], 71), 0)
    expert_ids = draw_expert_ids(jax.random.fold_in(seeds[12], 71), 0)
    norm_gain = jnp.clip(1.0 + 0.18 * jax.random.normal(seeds[7], (D,), jnp.float32), 0.1, 1.9)
    router_w = gaussian(seeds[8], (D, 2 * EXPERTS), D ** -0.5, 0.0625, ((0, 8),))
    w_in = draw_w_in(jax.random.fold_in(seeds[12], 71), 0)
    w_out = draw_w_out(jax.random.fold_in(seeds[12], 71), 0)
    grad_out = draw_grad_out(jax.random.fold_in(seeds[12], 71), 0)
    return dict(inputs=inputs, query_states=query_states, key_states=key_states, value_states=value_states, doc_ids=doc_ids, modality=modality, expert_ids=expert_ids, norm_gain=norm_gain, router_w=router_w, w_in=w_in, w_out=w_out, grad_out=grad_out)


eps_norm = 1e-05
gate_offset = 0.5

def gelu_back(pre_act, grad_in):
    return jax.vjp(lambda inner: jax.nn.gelu(inner, approximate=True), pre_act)[1](grad_in)[0]

def attention(query_states, key_states, value_states, doc_ids):
    group_size = HEADS // KV_HEADS
    query_heads = query_states.reshape(TOKENS, HEADS, HEAD_DIM).transpose(1, 0, 2)
    key_heads = key_states.reshape(TOKENS, KV_HEADS, HEAD_DIM).transpose(1, 0, 2)
    value_heads = value_states.reshape(TOKENS, KV_HEADS, HEAD_DIM).transpose(1, 0, 2)
    positions = jnp.arange(TOKENS, dtype=jnp.int32)
    allowed = (positions[None, :] <= positions[:, None]) & (doc_ids[None, :] == doc_ids[:, None])
    score_scale = HEAD_DIM ** (-0.5)

    def one_head(head_index):
        query_one = lax.dynamic_index_in_dim(query_heads, head_index, 0, keepdims=False)
        key_one = lax.dynamic_index_in_dim(key_heads, head_index // group_size, 0, keepdims=False)
        value_one = lax.dynamic_index_in_dim(value_heads, head_index // group_size, 0, keepdims=False)
        scores = jnp.dot(query_one, key_one.T, preferred_element_type=jnp.float32) * score_scale
        scores = jnp.where(allowed, scores, -1e+30)
        best_score = lax.optimization_barrier(jnp.max(scores, axis=1, keepdims=True))
        weights = jnp.where(allowed, jnp.exp(scores - best_score), 0.0)
        totals = lax.optimization_barrier(jnp.sum(weights, axis=1, keepdims=True))
        return jnp.dot(weights, value_one.astype(jnp.float32), precision=lax.Precision.HIGHEST) / totals
    head_out = lax.map(one_head, jnp.arange(HEADS, dtype=jnp.int32))
    return head_out.transpose(1, 0, 2).reshape(TOKENS, HEADS * HEAD_DIM).astype(jnp.bfloat16)

def expert_slots(modality, expert_ids):
    kept_mask = expert_ids >= 0
    column = modality[:, None] * EXPERTS + jnp.where(kept_mask, expert_ids, 0)
    one_hot = (column[:, :, None] == jnp.arange(2 * EXPERTS, dtype=jnp.int32)[None, None, :]) & kept_mask[:, :, None]
    counts = one_hot.astype(jnp.int32).reshape(N_SEQ, LEN_DEV * TOP, 2 * EXPERTS)
    earlier_count = jnp.cumsum(counts, axis=1) - counts
    slot_rank = lax.optimization_barrier(jnp.sum(earlier_count * counts, axis=2)).reshape(TOKENS, TOP)
    source = (jnp.arange(TOKENS, dtype=jnp.int32) // LEN_DEV)[:, None]
    slot_index = (column * N_SEQ + source) * CAP + slot_rank
    spare_row = 2 * EXPERTS * N_SEQ * CAP
    slot_index = jnp.where(kept_mask, slot_index, spare_row).astype(jnp.int32)
    return (kept_mask, one_hot, slot_index)

def fill_slots(entry_rows, slot_index):
    spare_row = 2 * EXPERTS * N_SEQ * CAP
    buffer = jnp.zeros((spare_row + 1, D), jnp.bfloat16)
    for choice_k in range(TOP):
        buffer = buffer.at[slot_index[:, choice_k]].set(entry_rows[choice_k])
    return buffer[:spare_row].reshape(2 * EXPERTS, N_SEQ * CAP, D)

def read_slots(buffer, slot_index):
    flat = jnp.concatenate([buffer.reshape(-1, D), jnp.zeros((1, D), jnp.bfloat16)], axis=0)
    return [flat[slot_index[:, choice_k]] for choice_k in range(TOP)]

def reference(inputs, query_states, key_states, value_states, doc_ids, modality, expert_ids, norm_gain, router_w, w_in, w_out, grad_out):
    attended = attention(query_states, key_states, value_states, doc_ids)
    resid_state = (inputs.astype(jnp.float32) + attended.astype(jnp.float32)).astype(jnp.bfloat16)
    state_wide = resid_state.astype(jnp.float32)
    inv_rms = lax.rsqrt(lax.optimization_barrier(jnp.mean(state_wide * state_wide, axis=1, keepdims=True)) + eps_norm)
    scaled = state_wide * norm_gain[None, :]
    normed = (scaled * inv_rms).astype(jnp.bfloat16)
    logits = jnp.dot(normed, router_w, preferred_element_type=jnp.float32)
    kept_mask, one_hot, slot_index = expert_slots(modality, expert_ids)
    kept_wide = kept_mask.astype(jnp.float32)
    chosen = lax.optimization_barrier(jnp.sum(jnp.where(one_hot, logits[:, None, :], 0.0), axis=2))
    lifted = jax.nn.sigmoid(chosen)
    denominator = gate_offset + lax.optimization_barrier(jnp.sum(kept_wide * lifted, axis=1, keepdims=True))
    gates = kept_wide * lifted / denominator
    slice_width = D // N_GRP
    w_in_all = w_in.reshape(2 * EXPERTS, D, FF)
    w_out_all = w_out.reshape(2 * EXPERTS, FF, D)
    sent_rows = fill_slots([normed] * TOP, slot_index)

    def forward_one(bundle):
        slot_rows, weight_in, weight_out = bundle
        partials = jnp.einsum('rgd,gdf->grf', slot_rows.reshape(-1, N_GRP, slice_width).astype(jnp.float32), weight_in.reshape(N_GRP, slice_width, FF).astype(jnp.float32))
        pre_act = lax.optimization_barrier(jnp.sum(lax.optimization_barrier(partials.astype(jnp.bfloat16)).astype(jnp.float32), axis=0))
        active = jax.nn.gelu(pre_act, approximate=True).astype(jnp.bfloat16)
        return (jnp.dot(active, weight_out, preferred_element_type=jnp.float32).astype(jnp.bfloat16), pre_act)
    expert_out, pre_all = lax.map(forward_one, (sent_rows, w_in_all, w_out_all))
    entry_out = read_slots(expert_out, slot_index)
    grad_wide = grad_out.astype(jnp.float32)
    mixture = jnp.zeros((TOKENS, D), jnp.float32)
    gate_cols = []
    for choice_k in range(TOP):
        out_wide = entry_out[choice_k].astype(jnp.float32)
        mixture = mixture + gates[:, choice_k:choice_k + 1] * out_wide
        gate_cols.append(lax.optimization_barrier(jnp.sum(grad_wide * out_wide, axis=1)))
    layer_out = (state_wide + mixture).astype(jnp.bfloat16)
    gate_grad = jnp.stack(gate_cols, axis=1)
    gate_dot = lax.optimization_barrier(jnp.sum(gates * gate_grad, axis=1, keepdims=True))
    logit_grad = kept_wide * (gate_grad - gate_dot) / denominator * lifted * (1.0 - lifted)
    logit_full = lax.optimization_barrier(jnp.sum(jnp.where(one_hot, logit_grad[:, :, None], 0.0), axis=1))
    router_grad = jnp.dot(logit_full, router_w.astype(jnp.float32).T, precision=lax.Precision.HIGHEST)
    grad_rows = [(gates[:, choice_k:choice_k + 1] * grad_wide).astype(jnp.bfloat16) for choice_k in range(TOP)]
    back_rows = fill_slots(grad_rows, slot_index)

    def backward_one(bundle):
        slot_rows, pre_act, weight_in, weight_out = bundle
        partials = jnp.einsum('rgd,fgd->grf', slot_rows.reshape(-1, N_GRP, slice_width).astype(jnp.float32), weight_out.reshape(FF, N_GRP, slice_width).astype(jnp.float32))
        act_grad = lax.optimization_barrier(jnp.sum(lax.optimization_barrier(partials.astype(jnp.bfloat16)).astype(jnp.float32), axis=0))
        pre_grad = gelu_back(pre_act, act_grad).astype(jnp.bfloat16)
        return jnp.dot(pre_grad, weight_in.T, preferred_element_type=jnp.float32).astype(jnp.bfloat16)
    entry_grad = lax.map(backward_one, (back_rows, pre_all, w_in_all, w_out_all))
    entry_back = read_slots(entry_grad, slot_index)
    normed_grad = router_grad
    for choice_k in range(TOP):
        normed_grad = normed_grad + entry_back[choice_k].astype(jnp.float32)
    norm_dot = lax.optimization_barrier(jnp.sum(normed_grad * scaled, axis=1, keepdims=True))
    state_grad = grad_wide + inv_rms * norm_gain[None, :] * normed_grad - inv_rms ** 3 / D * state_wide * norm_dot
    return (layer_out, state_grad.astype(jnp.bfloat16))
```

```python
import functools

import jax
import jax.numpy as jnp
from jax import lax
from jax.experimental import pallas as pl
from jax.experimental.pallas import tpu as pltpu
from jax.sharding import PartitionSpec as P

D = 8192
HEADS = 64
KV_HEADS = 8
HEAD_DIM = 128
FF = 1408
TOP = 4
CAP = 16
LEN = 128
WIDTH = 1024

eps_norm = 1e-05
gate_offset = 0.5

MESH = pl.DeviceIdType.MESH
VMEM = pl.BlockSpec(memory_space=pltpu.VMEM)
ANY = pl.BlockSpec(memory_space=pl.ANY)
LIMIT = 56 * 1024 * 1024


def params(collective_id=None):
    if collective_id is None:
        return pltpu.CompilerParams(vmem_limit_bytes=LIMIT)
    return pltpu.CompilerParams(
        collective_id=collective_id, has_side_effects=True, vmem_limit_bytes=LIMIT
    )


class Links:
    def __init__(self, send, recv):
        self.send, self.recv = send, recv
        self.used = 0
        self.started = []

    def ids(self, count):
        first = self.used
        self.used += count
        return [first + i for i in range(count)]

    def copy(self, src, dst, index, axis, peer):
        return pltpu.make_async_remote_copy(
            src_ref=src,
            dst_ref=dst,
            send_sem=self.send.at[index],
            recv_sem=self.recv.at[index],
            device_id={axis: peer},
            device_id_type=MESH,
        )

    def start(self, src, dst, index, axis, peer):
        copy = self.copy(src, dst, index, axis, peer)
        copy.start()
        self.started.append(copy)
        return copy

    def local(self, src, dst, index):
        copy = pltpu.make_async_copy(src, dst, self.send.at[index])
        copy.start()
        return copy

    def finish(self):
        for copy in self.started:
            copy.wait_send()


def greet(axis, peers):
    barrier = pltpu.get_barrier_semaphore()
    for peer in peers:
        pl.semaphore_signal(barrier, inc=1, device_id={axis: peer}, device_id_type=MESH)
    pl.semaphore_wait(barrier, len(peers))


class Place:
    def __init__(self):
        me = lax.axis_index("seq")
        self.y, self.rest = me // 8, me % 8
        self.z, self.x = self.rest // 4, self.rest % 4
        self.zp = self.at(z=1 - self.z)
        self.xr, self.xl = self.at(x=(self.x + 1) % 4), self.at(x=(self.x + 3) % 4)
        self.yr, self.yl = self.at(y=(self.y + 1) % 4), self.at(y=(self.y + 3) % 4)
        self.y_next, self.y_prev, self.y_far = (self.y + 1) % 4, (self.y + 3) % 4, (self.y + 2) % 4

    def at(self, y=None, z=None, x=None):
        y = self.y if y is None else y
        z = self.z if z is None else z
        x = self.x if x is None else x
        return y * 8 + z * 4 + x

    def block(self, z, shift):
        return z * 4 + (self.x + shift) % 4


def slot_codes(rest):
    row = lax.broadcasted_iota(jnp.int32, (LEN, LEN), 0)
    owner = (row // 32) * 8 + rest
    return (((row // 16) % 2) * 32 + owner) * CAP + row % 16


def kv_kernel(kv_in, kv_out, send, recv):
    here = Place()
    links = Links(send, recv)
    me = here.at()
    greet("seq", [here.zp, here.xr, here.xl, here.yr, here.yl])
    own_id, z_id = links.ids(2)
    x1r, x1l, x2r, x2l = links.ids(2), links.ids(2), links.ids(2), links.ids(2)
    yr_id, yl_id, f_id = links.ids(8), links.ids(8), links.ids(8)
    own = links.local(kv_in, kv_out.at[me], own_id)
    half = LEN // 2

    def spot(z, shift, y=None):
        return kv_out.at[here.at(y=y, z=z, x=(here.x + shift) % 4)]

    def y_send(order, src, dst):
        r = links.start(src, dst, yr_id[order], "seq", here.yr)
        l = links.start(src, dst, yl_id[order], "seq", here.yl)
        return r, l

    zc = links.start(kv_in, spot(here.z, 0), z_id, "seq", here.zp)
    sent = {}
    zs = [here.z, 1 - here.z]
    first = [None, None]
    second = [None, None]
    first[0] = (
        links.start(kv_in, spot(zs[0], 0), x1r[0], "seq", here.xr),
        links.start(kv_in, spot(zs[0], 0), x1l[0], "seq", here.xl),
    )
    sent[0] = y_send(0, kv_in, spot(zs[0], 0))

    def forward_x(p):
        z = zs[p]
        first[p][0].wait_recv()
        left = spot(z, 3)
        a = links.start(left.at[pl.ds(0, half)], left.at[pl.ds(0, half)], x2r[p], "seq", here.xr)
        sent[p * 4 + 1] = y_send(p * 4 + 1, left, left)
        first[p][1].wait_recv()
        right = spot(z, 1)
        b = links.start(
            right.at[pl.ds(half, half)], right.at[pl.ds(half, half)], x2l[p], "seq", here.xl
        )
        sent[p * 4 + 2] = y_send(p * 4 + 2, right, right)
        second[p] = (a, b)

    def far_x(p):
        second[p][0].wait_recv()
        second[p][1].wait_recv()
        far = spot(zs[p], 2)
        sent[p * 4 + 3] = y_send(p * 4 + 3, far, far)

    shifts = [0, 3, 1, 2]
    forwarded = []

    def forward_y(order):
        z, shift = zs[order // 4], shifts[order % 4]
        if order % 2 == 0:
            sent[order][0].wait_recv()
            piece = spot(z, shift, here.y_prev)
            forwarded.append(links.start(piece, piece, f_id[order], "seq", here.yr))
        else:
            sent[order][1].wait_recv()
            piece = spot(z, shift, here.y_next)
            forwarded.append(links.start(piece, piece, f_id[order], "seq", here.yl))

    forward_x(0)
    zc.wait_recv()
    other = spot(zs[1], 0)
    first[1] = (
        links.start(other, other, x1r[1], "seq", here.xr),
        links.start(other, other, x1l[1], "seq", here.xl),
    )
    sent[4] = y_send(4, other, other)
    forward_y(0)
    far_x(0)
    forward_y(1)
    forward_x(1)
    forward_y(2)
    far_x(1)
    for order in range(3, 8):
        forward_y(order)
    for order in range(8):
        sent[order][1 if order % 2 == 0 else 0].wait_recv()
    for copy in forwarded:
        copy.wait_recv()
    own.wait()
    links.finish()


KV_SEMS = 2 + 8 + 24


def gather_kv(kv):
    return pl.pallas_call(
        kv_kernel,
        name="gather_kv",
        out_shape=jax.ShapeDtypeStruct((32, LEN, 2 * HEAD_DIM), jnp.bfloat16),
        in_specs=[VMEM],
        out_specs=ANY,
        scratch_shapes=[pltpu.SemaphoreType.DMA((KV_SEMS,)), pltpu.SemaphoreType.DMA((KV_SEMS,))],
        compiler_params=params(0),
    )(kv)


def dispatch_kernel(share, *refs):
    if share:
        rows, slots, got, tokens, table, out_buf, far_buf, send, recv = refs
    else:
        rows, table, got, tokens, out_buf, far_buf, send, recv = refs
    here = Place()
    links = Links(send, recv)
    peers = [here.zp, here.xr, here.xl, here.yr, here.yl]
    if share:
        peers += [here.at(x=(here.x + 2) % 4)] + [
            here.at(z=1 - here.z, x=(here.x + shift) % 4) for shift in (1, 2, 3)
        ]
    zs = [here.z, 1 - here.z]
    shifts = [0, 3, 1, 2]
    half = LEN // 2
    (z_id,) = links.ids(1)
    x1r, x1l, x2r, x2l = links.ids(2), links.ids(2), links.ids(2), links.ids(2)
    yr_id, yl_id, f1_id, f2_id, own_id = (
        links.ids(8),
        links.ids(8),
        links.ids(8),
        links.ids(8),
        links.ids(8),
    )
    t_id = links.ids(8)
    greet("seq", peers)

    def spot(p, shift):
        return tokens.at[here.block(zs[p], shift)]

    mine = spot(0, 0)
    zc = links.start(rows, mine, z_id, "seq", here.zp)
    first = [None, None]
    second = [None, None]
    first[0] = (
        links.start(rows, mine, x1r[0], "seq", here.xr),
        links.start(rows, mine, x1l[0], "seq", here.xl),
    )
    if share:
        told = []
        for order in range(1, 8):
            peer = here.at(z=zs[order // 4], x=(here.x + shifts[order % 4]) % 4)
            told.append(
                links.start(slots, table.at[here.rest], t_id[order], "seq", peer)
            )
        table[here.rest] = slots[...]
    tokens[here.rest] = rows[...]
    codes = slot_codes(here.rest)
    sent = {}
    locals_ = []

    def pick(order):
        p, shift = order // 4, shifts[order % 4]
        block = here.block(zs[p], shift)
        ids = table[block]
        hot = jnp.zeros((LEN, LEN), jnp.float32)
        for k in range(TOP):
            hot = hot + jnp.where(ids[k : k + 1, :] == codes, 1.0, 0.0)
        picked = jnp.dot(
            hot.astype(jnp.bfloat16), tokens[block], preferred_element_type=jnp.float32
        )
        out_buf[:, :, block] = picked.astype(jnp.bfloat16).reshape(4, 2, CAP, WIDTH)
        place = got.at[:, here.y, block]
        a = links.start(
            out_buf.at[here.y_next, :, block], place, yr_id[order], "seq", here.yr
        )
        b = links.start(
            out_buf.at[here.y_prev, :, block], place, yl_id[order], "seq", here.yl
        )
        c = links.start(
            out_buf.at[here.y_far, :, block],
            far_buf.at[order],
            f1_id[order],
            "seq",
            here.yr if order % 2 == 0 else here.yl,
        )
        locals_.append(links.local(out_buf.at[here.y, :, block], place, own_id[order]))
        sent[order] = [a, b, c]

    def forward_y(order):
        p, shift = order // 4, shifts[order % 4]
        block = here.block(zs[p], shift)
        sent[order][2].wait_recv()
        source, target = (
            (here.y_prev, here.yr) if order % 2 == 0 else (here.y_next, here.yl)
        )
        sent[order].append(
            links.start(
                far_buf.at[order], got.at[:, source, block], f2_id[order], "seq", target
            )
        )

    def forward_x(p):
        first[p][0].wait_recv()
        left = spot(p, 3)
        a = links.start(left.at[pl.ds(0, half)], left.at[pl.ds(0, half)], x2r[p], "seq", here.xr)
        first[p][1].wait_recv()
        right = spot(p, 1)
        b = links.start(
            right.at[pl.ds(half, half)], right.at[pl.ds(half, half)], x2l[p], "seq", here.xl
        )
        second[p] = (a, b)

    def far_x(p):
        second[p][0].wait_recv()
        second[p][1].wait_recv()

    if share:
        for copy in told:
            copy.wait_recv()
    pick(0)
    forward_x(0)
    pick(1)
    pick(2)
    zc.wait_recv()
    other = spot(1, 0)
    first[1] = (
        links.start(other, other, x1r[1], "seq", here.xr),
        links.start(other, other, x1l[1], "seq", here.xl),
    )
    forward_y(0)
    pick(4)
    far_x(0)
    pick(3)
    forward_y(1)
    forward_y(2)
    forward_x(1)
    pick(5)
    pick(6)
    forward_y(4)
    forward_y(3)
    far_x(1)
    pick(7)
    for order in (5, 6, 7):
        forward_y(order)
    for order in range(8):
        sent[order][0].wait_recv()
        sent[order][1].wait_recv()
        sent[order][3].wait_recv()
    for copy in locals_:
        copy.wait()
    links.finish()


DISPATCH_SEMS = 1 + 8 + 40 + 8


def dispatch_first(rows, slots):
    return pl.pallas_call(
        functools.partial(dispatch_kernel, True),
        name="dispatch_grads",
        out_shape=(
            jax.ShapeDtypeStruct((2, 4, 8, CAP, WIDTH), jnp.bfloat16),
            jax.ShapeDtypeStruct((8, LEN, WIDTH), jnp.bfloat16),
            jax.ShapeDtypeStruct((8, 8, LEN), jnp.int32),
        ),
        in_specs=[VMEM, VMEM],
        out_specs=(ANY, VMEM, VMEM),
        scratch_shapes=[
            pltpu.VMEM((4, 2, 8, CAP, WIDTH), jnp.bfloat16),
            pltpu.VMEM((8, 2, CAP, WIDTH), jnp.bfloat16),
            pltpu.SemaphoreType.DMA((DISPATCH_SEMS,)),
            pltpu.SemaphoreType.DMA((DISPATCH_SEMS,)),
        ],
        compiler_params=params(1),
    )(rows, slots)


def dispatch_next(rows, table):
    return pl.pallas_call(
        functools.partial(dispatch_kernel, False),
        name="dispatch_rows",
        out_shape=jax.ShapeDtypeStruct((2, 4, 8, CAP, WIDTH), jnp.bfloat16),
        in_specs=[VMEM, VMEM],
        out_specs=ANY,
        scratch_shapes=[
            pltpu.VMEM((8, LEN, WIDTH), jnp.bfloat16),
            pltpu.VMEM((4, 2, 8, CAP, WIDTH), jnp.bfloat16),
            pltpu.VMEM((8, 2, CAP, WIDTH), jnp.bfloat16),
            pltpu.SemaphoreType.DMA((DISPATCH_SEMS,)),
            pltpu.SemaphoreType.DMA((DISPATCH_SEMS,)),
        ],
        compiler_params=params(2),
    )(rows, table)


def collect_kernel(forward, *refs):
    if forward:
        (
            results, table, gates, tokens, total, gates_all, gate_sum,
            back, part, far_buf, x_half, x_full, z_buf, grad_part, grad_got, send, recv,
        ) = refs
    else:
        (
            results, table, gates_all, total,
            back, part, far_buf, x_half, x_full, z_buf, send, recv,
        ) = refs
    here = Place()
    links = Links(send, recv)
    peers = [here.zp, here.xr, here.xl, here.yr, here.yl]
    if forward:
        peers += [here.at(x=(here.x + 2) % 4)] + [
            here.at(z=1 - here.z, x=(here.x + shift) % 4) for shift in (1, 2, 3)
        ]
    zs = [1 - here.z, here.z]
    shifts = [2, 1, 3, 0]
    half = LEN // 2
    (z_id,) = links.ids(1)
    hr, hl, fr, fl = links.ids(2), links.ids(2), links.ids(2), links.ids(2)
    yr_id, yl_id, f1_id, f2_id, own_id = (
        links.ids(8),
        links.ids(8),
        links.ids(8),
        links.ids(8),
        links.ids(8),
    )
    t_id, g_id = links.ids(8), links.ids(8)
    greet("seq", peers)
    blocks = [here.block(zs[order // 4], shifts[order % 4]) for order in range(8)]
    sent = {}
    locals_ = []
    for order in range(8):
        block = blocks[order]
        place = back.at[here.y, :, block]
        a = links.start(results.at[:, here.y_next, block], place, yr_id[order], "seq", here.yr)
        b = links.start(results.at[:, here.y_prev, block], place, yl_id[order], "seq", here.yl)
        c = links.start(
            results.at[:, here.y_far, block],
            far_buf.at[order],
            f1_id[order],
            "seq",
            here.yr if order % 2 == 0 else here.yl,
        )
        locals_.append(links.local(results.at[:, here.y, block], place, own_id[order]))
        sent[order] = [a, b, c]
    told = []
    if forward:
        for order in range(7):
            peer = here.at(z=zs[order // 4], x=(here.x + shifts[order % 4]) % 4)
            told.append(links.start(gates, gates_all.at[here.rest], t_id[order], "seq", peer))
        gates_all[here.rest] = gates[...]
        for copy in told:
            copy.wait_recv()
    codes = slot_codes(here.rest)

    def forward_y(order):
        sent[order][2].wait_recv()
        source, target = (
            (here.y_prev, here.yr) if order % 2 == 0 else (here.y_next, here.yl)
        )
        sent[order].append(
            links.start(
                far_buf.at[order], back.at[source, :, blocks[order]], f2_id[order], "seq", target
            )
        )

    grads_sent = []

    def combine(order):
        block = blocks[order]
        locals_[order].wait()
        for which in (0, 1, 3):
            sent[order][which].wait_recv()
        rows = back[:, :, block].reshape(LEN, WIDTH)
        ids = table[block]
        weight = gates_all[block]
        mix = jnp.zeros((LEN, LEN), jnp.float32)
        for k in range(TOP):
            mix = mix + jnp.where(ids[k : k + 1, :] == codes, weight[k : k + 1, :], 0.0)
        summed = lax.dot_general(
            mix.astype(jnp.bfloat16),
            rows,
            (((0,), (0,)), ((), ())),
            preferred_element_type=jnp.float32,
        )
        if forward:
            dots = lax.dot_general(
                rows, tokens[block], (((1,), (1,)), ((), ())), preferred_element_type=jnp.float32
            )
            for k in range(TOP):
                grad_part[order, k : k + 1, :] = jnp.sum(
                    jnp.where(ids[k : k + 1, :] == codes, dots, 0.0), axis=0, keepdims=True
                )
            grad_part[order, TOP:, :] = jnp.zeros((8 - TOP, LEN), jnp.float32)
            if order < 7:
                peer = here.at(z=zs[order // 4], x=(here.x + shifts[order % 4]) % 4)
                grads_sent.append(
                    links.start(
                        grad_part.at[order], grad_got.at[order], g_id[order], "seq", peer
                    )
                )
        return summed

    halves = [None, None]
    fulls = [[None, None], [None, None]]

    def far_step(p):
        block = blocks[p * 4]
        part[block] = combine(p * 4).astype(jnp.bfloat16)
        halves[p] = (
            links.start(
                part.at[block, pl.ds(0, half)], x_half.at[p, 0], hr[p], "seq", here.xr
            ),
            links.start(
                part.at[block, pl.ds(half, half)], x_half.at[p, 1], hl[p], "seq", here.xl
            ),
        )

    def near_step(p, side):
        order = p * 4 + 1 + side
        block = blocks[order]
        summed = combine(order)
        halves[p][side].wait_recv()
        arrived = x_half[p, side].astype(jnp.float32)
        low, high = summed[:half], summed[half:]
        if side == 0:
            low = low + arrived
        else:
            high = high + arrived
        part[block, pl.ds(0, half)] = low.astype(jnp.bfloat16)
        part[block, pl.ds(half, half)] = high.astype(jnp.bfloat16)
        fulls[p][side] = links.start(
            part.at[block],
            x_full.at[p, side],
            (fr if side == 0 else fl)[p],
            "seq",
            here.xr if side == 0 else here.xl,
        )

    def last_step(p):
        fulls[p][0].wait_recv()
        fulls[p][1].wait_recv()
        return x_full[p, 0].astype(jnp.float32) + x_full[p, 1].astype(jnp.float32)

    forward_y(0)
    forward_y(1)
    far_step(0)
    forward_y(2)
    near_step(0, 0)
    forward_y(3)
    near_step(0, 1)
    forward_y(4)
    part[blocks[3]] = combine(3).astype(jnp.bfloat16)
    forward_y(5)
    far_step(1)
    forward_y(6)
    part[blocks[3]] = (part[blocks[3]].astype(jnp.float32) + last_step(0)).astype(jnp.bfloat16)
    zc = links.start(part.at[blocks[3]], z_buf, z_id, "seq", here.zp)
    forward_y(7)
    near_step(1, 0)
    near_step(1, 1)
    total[...] = combine(7)
    total[...] = total[...] + last_step(1)
    zc.wait_recv()
    total[...] = total[...] + z_buf[...].astype(jnp.float32)
    if forward:
        gathered = grad_part[7]
        for copy in grads_sent:
            copy.wait_recv()
        for order in range(7):
            gathered = gathered + grad_got[order]
        gate_sum[...] = gathered
    links.finish()


COLLECT_SEMS = 1 + 8 + 40 + 16


def collect_scratch(forward):
    scratch = [
        pltpu.VMEM((4, 2, 8, CAP, WIDTH), jnp.bfloat16),
        pltpu.VMEM((8, LEN, WIDTH), jnp.bfloat16),
        pltpu.VMEM((8, 2, CAP, WIDTH), jnp.bfloat16),
        pltpu.VMEM((2, 2, LEN // 2, WIDTH), jnp.bfloat16),
        pltpu.VMEM((2, 2, LEN, WIDTH), jnp.bfloat16),
        pltpu.VMEM((LEN, WIDTH), jnp.bfloat16),
    ]
    if forward:
        scratch += [pltpu.VMEM((8, 8, LEN), jnp.float32), pltpu.VMEM((7, 8, LEN), jnp.float32)]
    return scratch + [
        pltpu.SemaphoreType.DMA((COLLECT_SEMS,)),
        pltpu.SemaphoreType.DMA((COLLECT_SEMS,)),
    ]


def collect_forward(results, table, gates, tokens):
    return pl.pallas_call(
        functools.partial(collect_kernel, True),
        name="collect_forward",
        out_shape=(
            jax.ShapeDtypeStruct((LEN, WIDTH), jnp.float32),
            jax.ShapeDtypeStruct((8, 8, LEN), jnp.float32),
            jax.ShapeDtypeStruct((8, LEN), jnp.float32),
        ),
        in_specs=[ANY, VMEM, VMEM, VMEM],
        out_specs=(VMEM, VMEM, VMEM),
        scratch_shapes=collect_scratch(True),
        compiler_params=params(3),
    )(results, table, gates, tokens)


def collect_backward(results, table, gates_all):
    return pl.pallas_call(
        functools.partial(collect_kernel, False),
        name="collect_backward",
        out_shape=jax.ShapeDtypeStruct((LEN, WIDTH), jnp.float32),
        in_specs=[ANY, VMEM, VMEM],
        out_specs=VMEM,
        scratch_shapes=collect_scratch(False),
        compiler_params=params(4),
    )(results, table, gates_all)


def small_sum_kernel(part, total, got, send, recv):
    me = lax.axis_index("grp")
    links = Links(send, recv)
    peers = [(me + shift) % 8 for shift in range(1, 8)]
    ids = links.ids(7)
    greet("grp", peers)
    copies = [
        links.start(part, got.at[me], ids[i], "grp", peers[i]) for i in range(7)
    ]
    got[me] = part[...]
    for copy in copies:
        copy.wait_recv()
    summed = got[0]
    for i in range(1, 8):
        summed = summed + got[i]
    total[...] = summed
    links.finish()


def small_sum(part, collective_id, name):
    shape = part.shape
    return pl.pallas_call(
        small_sum_kernel,
        name=name,
        out_shape=jax.ShapeDtypeStruct(shape, jnp.float32),
        in_specs=[VMEM],
        out_specs=VMEM,
        scratch_shapes=[
            pltpu.VMEM((8,) + shape, jnp.float32),
            pltpu.SemaphoreType.DMA((7,)),
            pltpu.SemaphoreType.DMA((7,)),
        ],
        compiler_params=params(collective_id),
    )(part)


CHUNK = 32
CHUNKS = 256 // CHUNK


def hidden_kernel(part, total, held, sibling, arrived, send, recv):
    me = lax.axis_index("grp")
    core, chip = me % 2, me // 2
    high = chip // 2
    depth = chip + high * (3 - 2 * chip)
    twin = chip * 2 + 1 - core
    inner = me + 2 - 4 * high
    outer = (me + 6 + 4 * high) % 8
    links = Links(send, recv)
    pair_id, chain_id, spread_id, share_id = (links.ids(2 * CHUNKS) for _ in range(4))
    outgoing, incoming = 1 - high, high
    barrier = pltpu.get_barrier_semaphore()
    for peer in (twin, inner):
        pl.semaphore_signal(barrier, inc=1, device_id={"grp": peer}, device_id_type=MESH)

    @pl.when(depth == 1)
    def _():
        pl.semaphore_signal(barrier, inc=1, device_id={"grp": outer}, device_id_type=MESH)
        pl.semaphore_wait(barrier, 3)

    @pl.when(depth == 0)
    def _():
        pl.semaphore_wait(barrier, 2)

    def local(stream, i):
        return pl.ds(pl.multiple_of(stream * 256 + i * CHUNK, CHUNK), CHUNK)

    def whole(half, stream, i):
        return pl.ds(pl.multiple_of(half * 512 + stream * 256 + i * CHUNK, CHUNK), CHUNK)

    def pair(stream, i):
        return links.copy(
            part.at[whole(1 - core, stream, i)],
            sibling.at[local(stream, i)],
            pair_id[0] + stream * CHUNKS + i,
            "grp",
            twin,
        )

    def chain(stream, i, peer):
        spot = local(stream, i)
        return links.copy(
            held.at[spot], arrived.at[spot], chain_id[0] + stream * CHUNKS + i, "grp", peer
        )

    def spread(stream, i, peer):
        spot = total.at[whole(core, stream, i)]
        return links.copy(spot, spot, spread_id[0] + stream * CHUNKS + i, "grp", peer)

    def share(stream, i):
        spot = total.at[whole(core, stream, i)]
        return links.copy(spot, spot, share_id[0] + stream * CHUNKS + i, "grp", twin)

    for i in range(CHUNKS):
        pair(outgoing, i).start()
        pair(incoming, i).start()

    def own_sum(stream, i):
        pair(stream, i).wait_recv()
        return part[whole(core, stream, i)].astype(jnp.float32) + sibling[
            local(stream, i)
        ].astype(jnp.float32)

    @pl.when(depth == 0)
    def _():
        for i in range(CHUNKS):
            held[local(outgoing, i)] = own_sum(outgoing, i).astype(jnp.bfloat16)
            chain(outgoing, i, inner).start()
        for i in range(CHUNKS):
            own = own_sum(incoming, i)
            chain(incoming, i, inner).wait_recv()
            total[whole(core, incoming, i)] = (
                own + arrived[local(incoming, i)].astype(jnp.float32)
            ).astype(jnp.bfloat16)
            spread(incoming, i, inner).start()
            share(incoming, i).start()
        for i in range(CHUNKS):
            spread(outgoing, i, inner).wait_recv()
            share(outgoing, i).start()
        for i in range(CHUNKS):
            chain(outgoing, i, inner).wait_send()
            spread(incoming, i, inner).wait_send()

    @pl.when(depth == 1)
    def _():
        def pass_on(stream, i, source, target):
            own = own_sum(stream, i)
            chain(stream, i, source).wait_recv()
            held[local(stream, i)] = (
                own + arrived[local(stream, i)].astype(jnp.float32)
            ).astype(jnp.bfloat16)
            chain(stream, i, target).start()

        def hand_out(stream, i, source, target):
            spread(stream, i, source).wait_recv()
            spread(stream, i, target).start()
            share(stream, i).start()

        for i in range(CHUNKS):
            pass_on(outgoing, i, outer, inner)
            pass_on(incoming, i, inner, outer)
        for i in range(CHUNKS):
            hand_out(incoming, i, outer, inner)
            hand_out(outgoing, i, inner, outer)
        for i in range(CHUNKS):
            chain(outgoing, i, inner).wait_send()
            chain(incoming, i, outer).wait_send()
            spread(incoming, i, inner).wait_send()
            spread(outgoing, i, outer).wait_send()

    for i in range(CHUNKS):
        for stream in (0, 1):
            pair(stream, i).wait_send()
            share(stream, i).wait()


def hidden_sum(part):
    sems = 8 * CHUNKS
    return pl.pallas_call(
        hidden_kernel,
        name="hidden_sum",
        out_shape=jax.ShapeDtypeStruct((1024, FF), jnp.bfloat16),
        in_specs=[VMEM],
        out_specs=VMEM,
        scratch_shapes=[
            pltpu.VMEM((512, FF), jnp.bfloat16),
            pltpu.VMEM((512, FF), jnp.bfloat16),
            pltpu.VMEM((512, FF), jnp.bfloat16),
            pltpu.SemaphoreType.DMA((sems,)),
            pltpu.SemaphoreType.DMA((sems,)),
        ],
        compiler_params=params(5),
    )(part)


KEYS = 512


def attend_kernel(bounds, query, kv, first_key, query_pos, inputs, resid, best, total, acc):
    scale = HEAD_DIM ** (-0.5) * 1.4426950408889634
    groups = HEADS // KV_HEADS
    best[...] = jnp.full(best.shape, -1e30, jnp.float32)
    total[...] = jnp.zeros(total.shape, jnp.float32)
    acc[...] = jnp.zeros(acc.shape, jnp.float32)

    def step(i, carry):
        start = pl.multiple_of(i * KEYS, KEYS)
        keys = kv[pl.ds(start, KEYS), pl.ds(0, HEAD_DIM)]
        values = kv[pl.ds(start, KEYS), pl.ds(HEAD_DIM, HEAD_DIM)]
        key_pos = start + lax.broadcasted_iota(jnp.int32, (LEN, KEYS), 1)
        allowed = (key_pos <= query_pos[...]) & (key_pos >= first_key[...])
        for h in range(groups):
            scores = lax.dot_general(
                query[:, h * HEAD_DIM : (h + 1) * HEAD_DIM],
                keys,
                (((1,), (1,)), ((), ())),
                preferred_element_type=jnp.float32,
            )
            scores = jnp.where(allowed, scores, -1e30)
            old = best[h]
            new = jnp.maximum(old, jnp.max(scores, axis=1, keepdims=True))
            weights = jnp.where(allowed, jnp.exp2((scores - new) * scale), 0.0)
            shrink = jnp.exp2((old - new) * scale)
            best[h] = new
            total[h] = total[h] * shrink + jnp.sum(weights, axis=1, keepdims=True)
            acc[h] = acc[h] * shrink + jnp.dot(
                weights.astype(jnp.bfloat16), values, preferred_element_type=jnp.float32
            )
        return carry

    lax.fori_loop(bounds[0], bounds[1], step, 0)
    for h in range(groups):
        cols = slice(h * HEAD_DIM, (h + 1) * HEAD_DIM)
        attended = (acc[h] / total[h]).astype(jnp.bfloat16).astype(jnp.float32)
        resid[:, cols] = (inputs[:, cols].astype(jnp.float32) + attended).astype(jnp.bfloat16)


def attend(query, kv, doc_ids, inputs):
    first_query = lax.axis_index("seq") * LEN
    query_pos = first_query + jnp.arange(LEN, dtype=jnp.int32)
    query_doc = lax.dynamic_slice_in_dim(doc_ids, first_query, LEN)
    first_key = jnp.sum(
        (doc_ids[None, :] < query_doc[:, None]).astype(jnp.int32), axis=1, keepdims=True
    )
    bounds = jnp.stack([first_key[0, 0] // KEYS, (first_query + LEN + KEYS - 1) // KEYS])
    groups = HEADS // KV_HEADS
    return pl.pallas_call(
        attend_kernel,
        name="attend",
        out_shape=jax.ShapeDtypeStruct((LEN, WIDTH), jnp.bfloat16),
        in_specs=[pl.BlockSpec(memory_space=pltpu.SMEM)] + [VMEM] * 5,
        out_specs=VMEM,
        scratch_shapes=[
            pltpu.VMEM((groups, LEN, 1), jnp.float32),
            pltpu.VMEM((groups, LEN, 1), jnp.float32),
            pltpu.VMEM((groups, LEN, HEAD_DIM), jnp.float32),
        ],
        compiler_params=params(),
    )(bounds.astype(jnp.int32), query, kv, first_key, query_pos[:, None], inputs)


def gelu_slope(pre_act):
    return jax.vjp(lambda inner: jax.nn.gelu(inner, approximate=True), pre_act)[1](
        jnp.ones_like(pre_act)
    )[0]


def body(
    inputs,
    query_states,
    key_states,
    value_states,
    doc_ids,
    modality,
    expert_ids,
    norm_gain,
    router_w,
    w_in,
    w_out,
    grad_out,
):
    length, width = inputs.shape
    experts = lax.axis_size("seq")
    kept_mask = expert_ids >= 0
    kept_wide = kept_mask.astype(jnp.float32)
    column = modality[:, None] * experts + jnp.where(kept_mask, expert_ids, 0)
    one_hot = (
        column[:, :, None] == jnp.arange(2 * experts, dtype=jnp.int32)[None, None, :]
    ) & kept_mask[:, :, None]
    entries = length * TOP
    flat_hot = one_hot.reshape(entries, 2 * experts).astype(jnp.bfloat16)
    entry_range = jnp.arange(entries, dtype=jnp.int32)
    earlier = (entry_range[:, None] > entry_range[None, :]).astype(jnp.bfloat16)
    before = jnp.dot(earlier, flat_hot, preferred_element_type=jnp.float32)
    slot_rank = jnp.sum(before * flat_hot.astype(jnp.float32), axis=1).astype(jnp.int32)
    slots = jnp.where(kept_mask, column * CAP + slot_rank.reshape(length, TOP), -1)
    slots = jnp.concatenate([slots.T, jnp.full((8 - TOP, length), -1, jnp.int32)], axis=0)

    w_in_local = w_in[:, 0]
    w_out_local = w_out[:, 0]

    got_grads, tokens_grad, table = dispatch_first(grad_out, slots)
    partial_back = jnp.einsum(
        "ukx,utx->ukt",
        got_grads.reshape(2, experts * CAP, width),
        w_out_local,
        preferred_element_type=jnp.float32,
    ).astype(jnp.bfloat16)
    act_grad = lax.psum(partial_back, "grp")

    kv = gather_kv(jnp.concatenate([key_states, value_states], axis=1))
    resid_state = attend(query_states, kv.reshape(experts * length, 2 * HEAD_DIM), doc_ids, inputs)
    state_wide = resid_state.astype(jnp.float32)
    scaled = state_wide * norm_gain[None, :]
    raw_part = lax.dot_general(
        router_w,
        scaled.astype(jnp.bfloat16),
        (((0,), (1,)), ((), ())),
        preferred_element_type=jnp.float32,
    )
    square_part = jnp.sum(state_wide * state_wide, axis=1)[None, :]
    stats = small_sum(
        jnp.concatenate([raw_part, square_part, jnp.zeros((7, length), jnp.float32)], axis=0),
        6,
        "sum_stats",
    )
    inv_row = lax.rsqrt(stats[2 * experts] / D + eps_norm)
    inv_rms = inv_row[:, None]
    raw_logits = stats[: 2 * experts].T
    logits = raw_logits * inv_rms
    normed = (scaled * inv_rms).astype(jnp.bfloat16)
    chosen = jnp.sum(jnp.where(one_hot, logits[:, None, :], 0.0), axis=2)
    lifted = jax.nn.sigmoid(chosen)
    denominator = gate_offset + jnp.sum(kept_wide * lifted, axis=1, keepdims=True)
    gates = kept_wide * lifted / denominator
    gates_t = jnp.concatenate([gates.T, jnp.zeros((8 - TOP, length), jnp.float32)], axis=0)

    got_rows = dispatch_next(normed, table)
    partial_value = jnp.einsum(
        "ohn,ons->ohs",
        got_rows.reshape(2, experts * CAP, width),
        w_in_local,
        preferred_element_type=jnp.float32,
    ).astype(jnp.bfloat16)
    pre_act = hidden_sum(partial_value.reshape(2 * experts * CAP, FF)).reshape(
        2, experts * CAP, FF
    )
    pre_wide = pre_act.astype(jnp.float32)
    active = jax.nn.gelu(pre_wide, approximate=True).astype(jnp.bfloat16)
    expert_out = jnp.einsum(
        "nuv,nvg->nug", active, w_out_local, preferred_element_type=jnp.float32
    ).astype(jnp.bfloat16)
    mixture, gates_all, gate_part = collect_forward(
        expert_out.reshape(2, 4, 8, CAP, width), table, gates_t, tokens_grad
    )
    layer_out = (state_wide + mixture).astype(jnp.bfloat16)

    pre_grad = (gelu_slope(pre_wide) * act_grad.astype(jnp.float32)).astype(jnp.bfloat16)
    entry_grad = jnp.einsum(
        "upj,uoj->upo", pre_grad, w_in_local, preferred_element_type=jnp.float32
    ).astype(jnp.bfloat16)
    entry_sum = collect_backward(entry_grad.reshape(2, 4, 8, CAP, width), table, gates_all)
    entry_dot = jnp.sum(entry_sum * scaled, axis=1)[None, :]
    row_index = jnp.arange(8, dtype=jnp.int32)[:, None]
    ends = small_sum(jnp.where(row_index == TOP, entry_dot, gate_part), 7, "sum_ends")
    gate_grad = ends[:TOP].T
    gate_dot = jnp.sum(gates * gate_grad, axis=1, keepdims=True)
    logit_grad = kept_wide * (gate_grad - gate_dot) / denominator * lifted * (1.0 - lifted)
    logit_full = jnp.sum(jnp.where(one_hot, logit_grad[:, :, None], 0.0), axis=1)
    router_grad = jnp.dot(
        logit_full, router_w.astype(jnp.float32).T, precision=lax.Precision.HIGHEST
    )
    norm_dot = ends[TOP][:, None] + jnp.sum(logit_full * raw_logits, axis=1, keepdims=True)
    normed_grad = router_grad + entry_sum
    state_grad = (
        grad_out.astype(jnp.float32)
        + inv_rms * norm_gain[None, :] * normed_grad
        - inv_rms**3 / D * state_wide * norm_dot
    )
    return (layer_out, state_grad.astype(jnp.bfloat16))


def solution(mesh):
    in_specs = (
        P("seq", "grp"),
        P("seq", "grp"),
        P("seq", "grp"),
        P("seq", "grp"),
        P(),
        P("seq"),
        P("seq", None),
        P("grp"),
        P("grp", None),
        P(None, "seq", "grp", None),
        P(None, "seq", None, "grp"),
        P("seq", "grp"),
    )
    out_specs = (P("seq", "grp"), P("seq", "grp"))
    return jax.shard_map(body, mesh=mesh, in_specs=in_specs, out_specs=out_specs, check_vma=False)
```

```python
import functools

import jax
import jax.numpy as jnp
from jax import lax
from jax.experimental import pallas as pl
from jax.experimental.pallas import tpu as pltpu
from jax.sharding import PartitionSpec as P

D = 8192
HEADS = 64
KV_HEADS = 8
HEAD_DIM = 128
FF = 1408
TOP = 4
CAP = 16
LEN = 128
WIDTH = 1024

eps_norm = 1e-05
gate_offset = 0.5

MESH = pl.DeviceIdType.MESH
VMEM = pl.BlockSpec(memory_space=pltpu.VMEM)
ANY = pl.BlockSpec(memory_space=pl.ANY)
LIMIT = 56 * 1024 * 1024


def params(collective_id=None):
    if collective_id is None:
        return pltpu.CompilerParams(vmem_limit_bytes=LIMIT)
    return pltpu.CompilerParams(
        collective_id=collective_id, has_side_effects=True, vmem_limit_bytes=LIMIT
    )


class Links:
    def __init__(self, send, recv):
        self.send, self.recv = send, recv
        self.used = 0
        self.started = []

    def ids(self, count):
        first = self.used
        self.used += count
        return [first + i for i in range(count)]

    def copy(self, src, dst, index, axis, peer):
        return pltpu.make_async_remote_copy(
            src_ref=src,
            dst_ref=dst,
            send_sem=self.send.at[index],
            recv_sem=self.recv.at[index],
            device_id={axis: peer},
            device_id_type=MESH,
        )

    def start(self, src, dst, index, axis, peer):
        copy = self.copy(src, dst, index, axis, peer)
        copy.start()
        self.started.append(copy)
        return copy

    def local(self, src, dst, index):
        copy = pltpu.make_async_copy(src, dst, self.send.at[index])
        copy.start()
        return copy

    def finish(self):
        for copy in self.started:
            copy.wait_send()


def greet(axis, peers):
    barrier = pltpu.get_barrier_semaphore()
    for peer in peers:
        pl.semaphore_signal(barrier, inc=1, device_id={axis: peer}, device_id_type=MESH)
    pl.semaphore_wait(barrier, len(peers))


class Flow:
    def __init__(self, which, half):
        me = lax.axis_index("seq")
        y, z, x = me // 8, (me % 8) // 4, me % 4
        self.me, self.z, self.which = me, z, which
        if which == 0:
            self.a, self.b, self.step_a, self.step_b = x, y, 1, 8
        else:
            self.a, self.b, self.step_a, self.step_b = y, x, 8, 1
        self.cols = pl.ds(which * half, half)
        self.home = z * 4 + self.a
        self.zp = self.at(z=1 - z)
        self.ar, self.al = self.at(da=1), self.at(da=3)
        self.br, self.bl = self.at(db=1), self.at(db=3)

    def at(self, z=None, da=0, db=0):
        z = self.z if z is None else z
        return z * 4 + ((self.a + da) % 4) * self.step_a + ((self.b + db) % 4) * self.step_b

    def row(self, db):
        return (self.b + db) % 4

    def block(self, z, da):
        return z * 4 + (self.a + da) % 4

    def codes(self):
        row = lax.broadcasted_iota(jnp.int32, (LEN, LEN), 0)
        owner = (row // 32) * self.step_b + self.z * 4 + self.a * self.step_a
        return (((row // 16) % 2) * 32 + owner) * CAP + row % 16

    def family(self):
        return [self.at(da=d) for d in (1, 2, 3)] + [
            self.at(z=1 - self.z, da=d) for d in (0, 1, 2, 3)
        ]


def near_peers(flow):
    return [flow.zp, flow.ar, flow.al, flow.br, flow.bl]


def all_peers(flow, other):
    return flow.family() + other.family()[:3] + other.family()[4:]


HALF = LEN // 2
SHIFTS = [0, 3, 1, 2]


class GatherStream:
    def __init__(self, links, flow, source, out):
        self.links, self.flow, self.out = links, flow, out
        self.source = source.at[:, flow.cols]
        self.zs = [flow.z, 1 - flow.z]
        self.own_id, self.z_id = links.ids(2)
        self.a1r, self.a1l, self.a2r, self.a2l = (links.ids(2) for _ in range(4))
        self.r_id, self.l_id, self.f_id = (links.ids(8) for _ in range(3))
        self.sent, self.first, self.second, self.far = {}, {}, {}, {}

    def spot(self, order, db=0, rows=None):
        flow = self.flow
        place = flow.at(z=self.zs[order // 4], da=SHIFTS[order % 4], db=db)
        rows = pl.ds(0, LEN) if rows is None else rows
        return self.out.at[place, rows, flow.cols]

    def piece(self, order):
        return self.source if order == 0 else self.spot(order)

    def begin(self):
        self.own = self.links.local(self.source, self.spot(0), self.own_id)
        self.zc = self.links.start(self.source, self.spot(0), self.z_id, "seq", self.flow.zp)
        self.send_a(0)

    def send_a(self, p):
        src, dst = self.piece(p * 4), self.spot(p * 4)
        self.first[p] = (
            self.links.start(src, dst, self.a1r[p], "seq", self.flow.ar),
            self.links.start(src, dst, self.a1l[p], "seq", self.flow.al),
        )

    def forward_a(self, p):
        low, high = pl.ds(0, HALF), pl.ds(HALF, HALF)
        self.first[p][0].wait_recv()
        left = self.spot(p * 4 + 1, rows=low)
        one = self.links.start(left, left, self.a2r[p], "seq", self.flow.ar)
        self.first[p][1].wait_recv()
        right = self.spot(p * 4 + 2, rows=high)
        two = self.links.start(right, right, self.a2l[p], "seq", self.flow.al)
        self.second[p] = (one, two)

    def far_a(self, p):
        self.second[p][0].wait_recv()
        self.second[p][1].wait_recv()

    def other_z(self):
        self.zc.wait_recv()
        self.send_a(1)

    def pick(self, order):
        src, dst = self.piece(order), self.spot(order)
        self.sent[order] = (
            self.links.start(src, dst, self.r_id[order], "seq", self.flow.br),
            self.links.start(src, dst, self.l_id[order], "seq", self.flow.bl),
        )

    def forward_b(self, order):
        right = order % 2 == 0
        self.sent[order][0 if right else 1].wait_recv()
        piece = self.spot(order, db=3 if right else 1)
        self.far[order] = self.links.start(
            piece, piece, self.f_id[order], "seq", self.flow.br if right else self.flow.bl
        )

    def finish(self):
        for order in range(8):
            self.sent[order][1 if order % 2 == 0 else 0].wait_recv()
            self.far[order].wait_recv()
        self.own.wait()


class DispatchStream:
    def __init__(self, links, flow, rows, tokens, table, out_buf, far_buf, got):
        k = flow.which
        self.links, self.flow, self.got = links, flow, got
        self.rows = rows.at[:, flow.cols]
        self.tokens, self.table = tokens.at[k], table.at[k]
        self.out_buf, self.far_buf = out_buf.at[k], far_buf.at[k]
        self.zs = [flow.z, 1 - flow.z]
        (self.z_id,) = links.ids(1)
        self.a1r, self.a1l, self.a2r, self.a2l = (links.ids(2) for _ in range(4))
        self.r_id, self.l_id, self.f1_id, self.f2_id, self.own_id = (
            links.ids(8) for _ in range(5)
        )
        self.sent, self.first, self.second, self.far, self.kept = {}, {}, {}, {}, []
        self.codes = flow.codes()

    def block(self, order):
        return self.flow.block(self.zs[order // 4], SHIFTS[order % 4])

    def begin(self):
        mine = self.tokens.at[self.flow.home]
        self.zc = self.links.start(self.rows, mine, self.z_id, "seq", self.flow.zp)
        self.send_a(0, self.rows)
        self.tokens[self.flow.home] = self.rows[...]

    def send_a(self, p, src=None):
        spot = self.tokens.at[self.block(p * 4)]
        src = spot if src is None else src
        self.first[p] = (
            self.links.start(src, spot, self.a1r[p], "seq", self.flow.ar),
            self.links.start(src, spot, self.a1l[p], "seq", self.flow.al),
        )

    def forward_a(self, p):
        self.first[p][0].wait_recv()
        left = self.tokens.at[self.block(p * 4 + 1), pl.ds(0, HALF)]
        one = self.links.start(left, left, self.a2r[p], "seq", self.flow.ar)
        self.first[p][1].wait_recv()
        right = self.tokens.at[self.block(p * 4 + 2), pl.ds(HALF, HALF)]
        two = self.links.start(right, right, self.a2l[p], "seq", self.flow.al)
        self.second[p] = (one, two)

    def far_a(self, p):
        self.second[p][0].wait_recv()
        self.second[p][1].wait_recv()

    def other_z(self):
        self.zc.wait_recv()
        self.send_a(1)

    def pick(self, order):
        flow, links = self.flow, self.links
        block = self.block(order)
        ids = self.table[block]
        hot = jnp.zeros((LEN, LEN), jnp.float32)
        for k in range(TOP):
            hot = hot + jnp.where(ids[k : k + 1, :] == self.codes, 1.0, 0.0)
        picked = jnp.dot(
            hot.astype(jnp.bfloat16), self.tokens[block], preferred_element_type=jnp.float32
        )
        self.out_buf[:, :, block] = picked.astype(jnp.bfloat16).reshape(4, 2, CAP, WIDTH // 2)
        source = flow.at(z=self.zs[order // 4], da=SHIFTS[order % 4])
        place = self.got.at[:, source, :, flow.cols]
        right = order % 2 == 0
        self.sent[order] = (
            links.start(
                self.out_buf.at[flow.row(2), :, block],
                self.far_buf.at[order],
                self.f1_id[order],
                "seq",
                flow.br if right else flow.bl,
            ),
            links.start(
                self.out_buf.at[flow.row(1), :, block], place, self.r_id[order], "seq", flow.br
            ),
            links.start(
                self.out_buf.at[flow.row(3), :, block], place, self.l_id[order], "seq", flow.bl
            ),
        )
        self.kept.append(
            links.local(self.out_buf.at[flow.b, :, block], place, self.own_id[order])
        )

    def forward_b(self, order):
        flow = self.flow
        right = order % 2 == 0
        self.sent[order][0].wait_recv()
        source = flow.at(
            z=self.zs[order // 4], da=SHIFTS[order % 4], db=3 if right else 1
        )
        self.far[order] = self.links.start(
            self.far_buf.at[order],
            self.got.at[:, source, :, flow.cols],
            self.f2_id[order],
            "seq",
            flow.br if right else flow.bl,
        )

    def finish(self):
        for order in range(8):
            self.sent[order][1].wait_recv()
            self.sent[order][2].wait_recv()
            self.far[order].wait_recv()
        for copy in self.kept:
            copy.wait()


def run_streams(streams):
    def do(name, *given):
        for stream in streams:
            getattr(stream, name)(*given)

    do("pick", 0)
    do("forward_a", 0)
    do("pick", 1)
    do("pick", 2)
    do("other_z")
    do("forward_b", 0)
    do("pick", 4)
    do("far_a", 0)
    do("pick", 3)
    do("forward_b", 1)
    do("forward_b", 2)
    do("forward_a", 1)
    do("pick", 5)
    do("pick", 6)
    do("forward_b", 4)
    do("forward_b", 3)
    do("far_a", 1)
    do("pick", 7)
    for order in (5, 6, 7):
        do("forward_b", order)
    do("finish")


def tell(links, flow, ids, value, out):
    copies = [
        links.start(value, out.at[flow.home], ids[i], "seq", peer)
        for i, peer in enumerate(flow.family())
    ]
    out[flow.home] = value[...]
    return copies


def first_kernel(
    rows, slots, kv_in, got, tokens, table, kv_out, out_buf, far_buf, send, recv
):
    flows = [Flow(0, WIDTH // 2), Flow(1, WIDTH // 2)]
    kv_flows = [Flow(0, HEAD_DIM), Flow(1, HEAD_DIM)]
    links = Links(send, recv)
    greet("seq", all_peers(*flows))
    gathers = [GatherStream(links, flow, kv_in, kv_out) for flow in kv_flows]
    streams = [
        DispatchStream(links, flow, rows, tokens, table, out_buf, far_buf, got) for flow in flows
    ]
    told = []
    for flow in flows:
        told += tell(links, flow, links.ids(7), slots, table.at[flow.which])
    for stream in gathers + streams:
        stream.begin()
    for copy in told:
        copy.wait_recv()
    run_streams(gathers + streams)
    links.finish()


FIRST_SEMS = 2 * 34 + 2 * 49 + 14


def dispatch_first(rows, slots, kv):
    return pl.pallas_call(
        first_kernel,
        name="dispatch_grads",
        out_shape=(
            jax.ShapeDtypeStruct((2, 32, CAP, WIDTH), jnp.bfloat16),
            jax.ShapeDtypeStruct((2, 8, LEN, WIDTH // 2), jnp.bfloat16),
            jax.ShapeDtypeStruct((2, 8, 8, LEN), jnp.int32),
            jax.ShapeDtypeStruct((32, LEN, 2 * HEAD_DIM), jnp.bfloat16),
        ),
        in_specs=[VMEM, VMEM, VMEM],
        out_specs=(ANY, VMEM, VMEM, ANY),
        scratch_shapes=[
            pltpu.VMEM((2, 4, 2, 8, CAP, WIDTH // 2), jnp.bfloat16),
            pltpu.VMEM((2, 8, 2, CAP, WIDTH // 2), jnp.bfloat16),
            pltpu.SemaphoreType.DMA((FIRST_SEMS,)),
            pltpu.SemaphoreType.DMA((FIRST_SEMS,)),
        ],
        compiler_params=params(1),
    )(rows, slots, kv)


def next_kernel(rows, table, got, tokens, out_buf, far_buf, send, recv):
    flows = [Flow(0, WIDTH // 2), Flow(1, WIDTH // 2)]
    links = Links(send, recv)
    greet("seq", near_peers(flows[0]))
    streams = [
        DispatchStream(links, flow, rows, tokens, table, out_buf, far_buf, got) for flow in flows
    ]
    for stream in streams:
        stream.begin()
    run_streams(streams)
    links.finish()


def dispatch_next(rows, table):
    return pl.pallas_call(
        next_kernel,
        name="dispatch_rows",
        out_shape=jax.ShapeDtypeStruct((2, 32, CAP, WIDTH), jnp.bfloat16),
        in_specs=[VMEM, VMEM],
        out_specs=ANY,
        scratch_shapes=[
            pltpu.VMEM((2, 8, LEN, WIDTH // 2), jnp.bfloat16),
            pltpu.VMEM((2, 4, 2, 8, CAP, WIDTH // 2), jnp.bfloat16),
            pltpu.VMEM((2, 8, 2, CAP, WIDTH // 2), jnp.bfloat16),
            pltpu.SemaphoreType.DMA((98,)),
            pltpu.SemaphoreType.DMA((98,)),
        ],
        compiler_params=params(2),
    )(rows, table)


BACK_SHIFTS = [2, 1, 3, 0]


class CollectStream:
    def __init__(self, links, flow, slot, results, scratch, total):
        self.links, self.flow, self.results = links, flow, results
        self.back, self.part, self.far_buf, self.a_half, self.a_full, self.z_buf = (
            ref.at[slot] for ref in scratch
        )
        self.total = total.at[:, flow.cols]
        self.zs = [1 - flow.z, flow.z]
        (self.z_id,) = links.ids(1)
        self.hr, self.hl, self.fr, self.fl = (links.ids(2) for _ in range(4))
        self.r_id, self.l_id, self.f1_id, self.f2_id, self.own_id = (
            links.ids(8) for _ in range(5)
        )
        self.sent, self.far, self.kept, self.halves, self.fulls = {}, {}, {}, {}, {}

    def block(self, order):
        return self.flow.block(self.zs[order // 4], BACK_SHIFTS[order % 4])

    def piece(self, order, db):
        source = self.flow.at(z=self.zs[order // 4], da=BACK_SHIFTS[order % 4], db=db)
        return self.results.at[:, source, :, self.flow.cols]

    def begin(self, order):
        flow, links = self.flow, self.links
        block = self.block(order)
        place = self.back.at[flow.b, :, block]
        right = order % 2 == 0
        self.sent[order] = (
            links.start(
                self.piece(order, 2),
                self.far_buf.at[order],
                self.f1_id[order],
                "seq",
                flow.br if right else flow.bl,
            ),
            links.start(self.piece(order, 1), place, self.r_id[order], "seq", flow.br),
            links.start(self.piece(order, 3), place, self.l_id[order], "seq", flow.bl),
        )
        self.kept[order] = links.local(self.piece(order, 0), place, self.own_id[order])

    def forward_b(self, order):
        flow = self.flow
        right = order % 2 == 0
        self.sent[order][0].wait_recv()
        self.far[order] = self.links.start(
            self.far_buf.at[order],
            self.back.at[flow.row(3 if right else 1), :, self.block(order)],
            self.f2_id[order],
            "seq",
            flow.br if right else flow.bl,
        )

    def arrive(self, order):
        self.kept[order].wait()
        self.sent[order][1].wait_recv()
        self.sent[order][2].wait_recv()
        self.far[order].wait_recv()
        return self.back[:, :, self.block(order)].reshape(LEN, WIDTH // 2)

    def add_on(self, order, summed):
        p, step = order // 4, order % 4
        links, flow = self.links, self.flow
        part = self.part.at[self.block(order)]
        low, high = pl.ds(0, HALF), pl.ds(HALF, HALF)
        if step == 0:
            part[...] = summed.astype(jnp.bfloat16)
            self.halves[p] = (
                links.start(part.at[low], self.a_half.at[p, 0], self.hr[p], "seq", flow.ar),
                links.start(part.at[high], self.a_half.at[p, 1], self.hl[p], "seq", flow.al),
            )
        elif step in (1, 2):
            side = step - 1
            self.halves[p][side].wait_recv()
            arrived = self.a_half[p, side].astype(jnp.float32)
            top, bottom = summed[:HALF], summed[HALF:]
            if side == 0:
                top = top + arrived
            else:
                bottom = bottom + arrived
            part[low] = top.astype(jnp.bfloat16)
            part[high] = bottom.astype(jnp.bfloat16)
            self.fulls[p, side] = links.start(
                part,
                self.a_full.at[p, side],
                (self.fr if side == 0 else self.fl)[p],
                "seq",
                flow.ar if side == 0 else flow.al,
            )
        elif p == 0:
            part[...] = summed.astype(jnp.bfloat16)
        else:
            self.total[...] = summed

    def line_sum(self, p):
        self.fulls[p, 0].wait_recv()
        self.fulls[p, 1].wait_recv()
        return self.a_full[p, 0].astype(jnp.float32) + self.a_full[p, 1].astype(jnp.float32)

    def send_z(self):
        part = self.part.at[self.block(3)]
        part[...] = (part[...].astype(jnp.float32) + self.line_sum(0)).astype(jnp.bfloat16)
        self.zc = self.links.start(part, self.z_buf, self.z_id, "seq", self.flow.zp)

    def finish(self):
        self.total[...] = self.total[...] + self.line_sum(1)
        self.zc.wait_recv()
        self.total[...] = self.total[...] + self.z_buf[...].astype(jnp.float32)


def collect_kernel(
    results, back_results, table, gates, tokens, total, back_total, gate_sum,
    gates_all, back, part, far_buf, a_half, a_full, z_buf, grad_part, grad_got, send, recv,
):
    flows = [Flow(0, WIDTH // 2), Flow(1, WIDTH // 2)]
    links = Links(send, recv)
    greet("seq", all_peers(*flows))
    scratch = (back, part, far_buf, a_half, a_full, z_buf)
    pairs = [
        [
            CollectStream(links, flow, flow.which, results, scratch, total),
            CollectStream(links, flow, 2 + flow.which, back_results, scratch, back_total),
        ]
        for flow in flows
    ]
    streams = [pairs[0][0], pairs[1][0], pairs[0][1], pairs[1][1]]
    told = []
    for flow in flows:
        told += tell(links, flow, links.ids(7), gates, gates_all.at[flow.which])
    for order in range(8):
        for stream in streams:
            stream.begin(order)
    for copy in told:
        copy.wait_recv()
    codes = [flow.codes() for flow in flows]
    g_id = [links.ids(8), links.ids(8)]
    grads_sent = []

    def do(name, *given):
        for stream in streams:
            getattr(stream, name)(*given)

    def combine(order):
        for flow in flows:
            k = flow.which
            forward, backward = pairs[k]
            block = forward.block(order)
            ids, weight = table[k, block], gates_all[k, block]
            mix = jnp.zeros((LEN, LEN), jnp.float32)
            for c in range(TOP):
                mix = mix + jnp.where(ids[c : c + 1, :] == codes[k], weight[c : c + 1, :], 0.0)
            mix = mix.astype(jnp.bfloat16)
            for stream in (forward, backward):
                rows = stream.arrive(order)
                summed = lax.dot_general(
                    mix, rows, (((0,), (0,)), ((), ())), preferred_element_type=jnp.float32
                )
                stream.add_on(order, summed)
                if stream is backward:
                    continue
                dots = lax.dot_general(
                    rows,
                    tokens[k, block],
                    (((1,), (1,)), ((), ())),
                    preferred_element_type=jnp.float32,
                )
                for c in range(TOP):
                    grad_part[k, order, c : c + 1, :] = jnp.sum(
                        jnp.where(ids[c : c + 1, :] == codes[k], dots, 0.0),
                        axis=0,
                        keepdims=True,
                    )
                grad_part[k, order, TOP:, :] = jnp.zeros((8 - TOP, LEN), jnp.float32)
                if order < 7:
                    peer = flow.at(z=forward.zs[order // 4], da=BACK_SHIFTS[order % 4])
                    grads_sent.append(
                        links.start(
                            grad_part.at[k, order],
                            grad_got.at[k, order],
                            g_id[k][order],
                            "seq",
                            peer,
                        )
                    )

    do("forward_b", 0)
    do("forward_b", 1)
    combine(0)
    do("forward_b", 2)
    combine(1)
    do("forward_b", 3)
    combine(2)
    do("forward_b", 4)
    combine(3)
    do("forward_b", 5)
    combine(4)
    do("send_z")
    do("forward_b", 6)
    do("forward_b", 7)
    combine(5)
    combine(6)
    combine(7)
    do("finish")
    gathered = grad_part[0, 7] + grad_part[1, 7]
    for copy in grads_sent:
        copy.wait_recv()
    for k in range(2):
        for order in range(7):
            gathered = gathered + grad_got[k, order]
    gate_sum[...] = gathered
    links.finish()


COLLECT_SEMS = 4 * 49 + 14 + 16


def collect(results, back_results, table, gates, tokens):
    half = WIDTH // 2
    return pl.pallas_call(
        collect_kernel,
        name="collect",
        out_shape=(
            jax.ShapeDtypeStruct((LEN, WIDTH), jnp.float32),
            jax.ShapeDtypeStruct((LEN, WIDTH), jnp.float32),
            jax.ShapeDtypeStruct((8, LEN), jnp.float32),
        ),
        in_specs=[ANY, ANY, VMEM, VMEM, VMEM],
        out_specs=(VMEM, VMEM, VMEM),
        scratch_shapes=[
            pltpu.VMEM((2, 8, 8, LEN), jnp.float32),
            pltpu.VMEM((4, 4, 2, 8, CAP, half), jnp.bfloat16),
            pltpu.VMEM((4, 8, LEN, half), jnp.bfloat16),
            pltpu.VMEM((4, 8, 2, CAP, half), jnp.bfloat16),
            pltpu.VMEM((4, 2, 2, HALF, half), jnp.bfloat16),
            pltpu.VMEM((4, 2, 2, LEN, half), jnp.bfloat16),
            pltpu.VMEM((4, LEN, half), jnp.bfloat16),
            pltpu.VMEM((2, 8, 8, LEN), jnp.float32),
            pltpu.VMEM((2, 7, 8, LEN), jnp.float32),
            pltpu.SemaphoreType.DMA((COLLECT_SEMS,)),
            pltpu.SemaphoreType.DMA((COLLECT_SEMS,)),
        ],
        compiler_params=params(3),
    )(results, back_results, table, gates, tokens)


def small_sum_kernel(part, total, got, send, recv):
    me = lax.axis_index("grp")
    links = Links(send, recv)
    peers = [(me + shift) % 8 for shift in range(1, 8)]
    ids = links.ids(7)
    greet("grp", peers)
    copies = [
        links.start(part, got.at[me], ids[i], "grp", peers[i]) for i in range(7)
    ]
    got[me] = part[...]
    for copy in copies:
        copy.wait_recv()
    summed = got[0]
    for i in range(1, 8):
        summed = summed + got[i]
    total[...] = summed
    links.finish()


def small_sum(part, collective_id, name):
    shape = part.shape
    return pl.pallas_call(
        small_sum_kernel,
        name=name,
        out_shape=jax.ShapeDtypeStruct(shape, jnp.float32),
        in_specs=[VMEM],
        out_specs=VMEM,
        scratch_shapes=[
            pltpu.VMEM((8,) + shape, jnp.float32),
            pltpu.SemaphoreType.DMA((7,)),
            pltpu.SemaphoreType.DMA((7,)),
        ],
        compiler_params=params(collective_id),
    )(part)


CHUNK = 32
CHUNKS = 256 // CHUNK


def hidden_kernel(part, total, held, sibling, arrived, send, recv):
    me = lax.axis_index("grp")
    core, chip = me % 2, me // 2
    high = chip // 2
    depth = chip + high * (3 - 2 * chip)
    twin = chip * 2 + 1 - core
    inner = me + 2 - 4 * high
    outer = (me + 6 + 4 * high) % 8
    links = Links(send, recv)
    pair_id, chain_id, spread_id, share_id = (links.ids(2 * CHUNKS) for _ in range(4))
    outgoing, incoming = 1 - high, high
    barrier = pltpu.get_barrier_semaphore()
    for peer in (twin, inner):
        pl.semaphore_signal(barrier, inc=1, device_id={"grp": peer}, device_id_type=MESH)

    @pl.when(depth == 1)
    def _():
        pl.semaphore_signal(barrier, inc=1, device_id={"grp": outer}, device_id_type=MESH)
        pl.semaphore_wait(barrier, 3)

    @pl.when(depth == 0)
    def _():
        pl.semaphore_wait(barrier, 2)

    def local(stream, i):
        return pl.ds(pl.multiple_of(stream * 256 + i * CHUNK, CHUNK), CHUNK)

    def whole(half, stream, i):
        return pl.ds(pl.multiple_of(half * 512 + stream * 256 + i * CHUNK, CHUNK), CHUNK)

    def pair(stream, i):
        return links.copy(
            part.at[whole(1 - core, stream, i)],
            sibling.at[local(stream, i)],
            pair_id[0] + stream * CHUNKS + i,
            "grp",
            twin,
        )

    def chain(stream, i, peer):
        spot = local(stream, i)
        return links.copy(
            held.at[spot], arrived.at[spot], chain_id[0] + stream * CHUNKS + i, "grp", peer
        )

    def spread(stream, i, peer):
        spot = total.at[whole(core, stream, i)]
        return links.copy(spot, spot, spread_id[0] + stream * CHUNKS + i, "grp", peer)

    def share(stream, i):
        spot = total.at[whole(core, stream, i)]
        return links.copy(spot, spot, share_id[0] + stream * CHUNKS + i, "grp", twin)

    for i in range(CHUNKS):
        pair(outgoing, i).start()
        pair(incoming, i).start()

    def own_sum(stream, i):
        pair(stream, i).wait_recv()
        return part[whole(core, stream, i)].astype(jnp.float32) + sibling[
            local(stream, i)
        ].astype(jnp.float32)

    @pl.when(depth == 0)
    def _():
        for i in range(CHUNKS):
            held[local(outgoing, i)] = own_sum(outgoing, i).astype(jnp.bfloat16)
            chain(outgoing, i, inner).start()
        for i in range(CHUNKS):
            own = own_sum(incoming, i)
            chain(incoming, i, inner).wait_recv()
            total[whole(core, incoming, i)] = (
                own + arrived[local(incoming, i)].astype(jnp.float32)
            ).astype(jnp.bfloat16)
            spread(incoming, i, inner).start()
            share(incoming, i).start()
        for i in range(CHUNKS):
            spread(outgoing, i, inner).wait_recv()
            share(outgoing, i).start()
        for i in range(CHUNKS):
            chain(outgoing, i, inner).wait_send()
            spread(incoming, i, inner).wait_send()

    @pl.when(depth == 1)
    def _():
        def pass_on(stream, i, source, target):
            own = own_sum(stream, i)
            chain(stream, i, source).wait_recv()
            held[local(stream, i)] = (
                own + arrived[local(stream, i)].astype(jnp.float32)
            ).astype(jnp.bfloat16)
            chain(stream, i, target).start()

        def hand_out(stream, i, source, target):
            spread(stream, i, source).wait_recv()
            spread(stream, i, target).start()
            share(stream, i).start()

        for i in range(CHUNKS):
            pass_on(outgoing, i, outer, inner)
            pass_on(incoming, i, inner, outer)
        for i in range(CHUNKS):
            hand_out(incoming, i, outer, inner)
            hand_out(outgoing, i, inner, outer)
        for i in range(CHUNKS):
            chain(outgoing, i, inner).wait_send()
            chain(incoming, i, outer).wait_send()
            spread(incoming, i, inner).wait_send()
            spread(outgoing, i, outer).wait_send()

    for i in range(CHUNKS):
        for stream in (0, 1):
            pair(stream, i).wait_send()
            share(stream, i).wait()


def hidden_sum(part):
    sems = 8 * CHUNKS
    return pl.pallas_call(
        hidden_kernel,
        name="hidden_sum",
        out_shape=jax.ShapeDtypeStruct((1024, FF), jnp.bfloat16),
        in_specs=[VMEM],
        out_specs=VMEM,
        scratch_shapes=[
            pltpu.VMEM((512, FF), jnp.bfloat16),
            pltpu.VMEM((512, FF), jnp.bfloat16),
            pltpu.VMEM((512, FF), jnp.bfloat16),
            pltpu.SemaphoreType.DMA((sems,)),
            pltpu.SemaphoreType.DMA((sems,)),
        ],
        compiler_params=params(5),
    )(part)


KEYS = 512


def attend_kernel(bounds, query, kv, first_key, query_pos, inputs, resid, best, total, acc):
    scale = HEAD_DIM ** (-0.5) * 1.4426950408889634
    groups = HEADS // KV_HEADS
    best[...] = jnp.full(best.shape, -1e30, jnp.float32)
    total[...] = jnp.zeros(total.shape, jnp.float32)
    acc[...] = jnp.zeros(acc.shape, jnp.float32)

    def step(masked, i, carry):
        start = pl.multiple_of(i * KEYS, KEYS)
        keys = kv[pl.ds(start, KEYS), pl.ds(0, HEAD_DIM)]
        values = kv[pl.ds(start, KEYS), pl.ds(HEAD_DIM, HEAD_DIM)]
        if masked:
            key_pos = start + lax.broadcasted_iota(jnp.int32, (LEN, KEYS), 1)
            allowed = (key_pos <= query_pos[...]) & (key_pos >= first_key[...])
        for h in range(groups):
            scores = lax.dot_general(
                query[:, h * HEAD_DIM : (h + 1) * HEAD_DIM],
                keys,
                (((1,), (1,)), ((), ())),
                preferred_element_type=jnp.float32,
            )
            if masked:
                scores = jnp.where(allowed, scores, -1e30)
            old = best[h]
            new = jnp.maximum(old, jnp.max(scores, axis=1, keepdims=True))
            weights = jnp.exp2((scores - new) * scale)
            shrink = jnp.exp2((old - new) * scale)
            best[h] = new
            total[h] = total[h] * shrink + jnp.sum(weights, axis=1, keepdims=True)
            acc[h] = acc[h] * shrink + jnp.dot(
                weights.astype(jnp.bfloat16), values, preferred_element_type=jnp.float32
            )
        return carry

    lax.fori_loop(bounds[0], bounds[1], functools.partial(step, True), 0)
    lax.fori_loop(bounds[1], bounds[2], functools.partial(step, False), 0)
    lax.fori_loop(bounds[2], bounds[3], functools.partial(step, True), 0)
    for h in range(groups):
        cols = slice(h * HEAD_DIM, (h + 1) * HEAD_DIM)
        attended = (acc[h] / total[h]).astype(jnp.bfloat16).astype(jnp.float32)
        resid[:, cols] = (inputs[:, cols].astype(jnp.float32) + attended).astype(jnp.bfloat16)


def attend(query, kv, doc_ids, inputs):
    first_query = lax.axis_index("seq") * LEN
    query_pos = first_query + jnp.arange(LEN, dtype=jnp.int32)
    query_doc = lax.dynamic_slice_in_dim(doc_ids, first_query, LEN)
    first_key = jnp.sum(
        (doc_ids[None, :] < query_doc[:, None]).astype(jnp.int32), axis=1, keepdims=True
    )
    low = first_key[0, 0] // KEYS
    high = (first_query + LEN + KEYS - 1) // KEYS
    full_low = jnp.minimum((first_key[LEN - 1, 0] + KEYS - 1) // KEYS, high)
    full_high = jnp.maximum((first_query + 1) // KEYS, full_low)
    bounds = jnp.stack([low, full_low, full_high, high])
    groups = HEADS // KV_HEADS
    return pl.pallas_call(
        attend_kernel,
        name="attend",
        out_shape=jax.ShapeDtypeStruct((LEN, WIDTH), jnp.bfloat16),
        in_specs=[pl.BlockSpec(memory_space=pltpu.SMEM)] + [VMEM] * 5,
        out_specs=VMEM,
        scratch_shapes=[
            pltpu.VMEM((groups, LEN, 1), jnp.float32),
            pltpu.VMEM((groups, LEN, 1), jnp.float32),
            pltpu.VMEM((groups, LEN, HEAD_DIM), jnp.float32),
        ],
        compiler_params=params(),
    )(bounds.astype(jnp.int32), query, kv, first_key, query_pos[:, None], inputs)


def product_kernel(turned, rows, weight, out):
    out[0] = lax.dot_general(
        rows[0],
        weight[0],
        (((1,), (1 if turned else 0,)), ((), ())),
        preferred_element_type=jnp.float32,
    ).astype(jnp.bfloat16)


def product(rows, weight, turned, name):
    sets, count, depth = rows.shape
    width = weight.shape[1 if turned else 2]
    return pl.pallas_call(
        functools.partial(product_kernel, turned),
        name=name,
        grid=(sets,),
        out_shape=jax.ShapeDtypeStruct((sets, count, width), jnp.bfloat16),
        in_specs=[
            pl.BlockSpec((1, count, depth), lambda m: (m, 0, 0)),
            pl.BlockSpec((1,) + weight.shape[1:], lambda m: (m, 0, 0)),
        ],
        out_specs=pl.BlockSpec((1, count, width), lambda m: (m, 0, 0)),
        compiler_params=params(),
        cost_estimate=pl.CostEstimate(
            flops=2 * sets * count * depth * width,
            bytes_accessed=2 * sets * (count * depth + depth * width + count * width),
            transcendentals=0,
        ),
    )(rows, weight)


def expert_kernel(pre, act_grad, w_out, w_in, out, grad):
    root = 0.7978845608028654
    wide = pre[0].astype(jnp.float32)
    square = wide * wide
    curve = jnp.tanh(root * wide * (1.0 + 0.044715 * square))
    active = (0.5 * wide * (1.0 + curve)).astype(jnp.bfloat16)
    out[0] = jnp.dot(active, w_out[0], preferred_element_type=jnp.float32).astype(jnp.bfloat16)
    slope = 0.5 * (1.0 + curve) + (0.5 * root) * wide * (1.0 - curve * curve) * (
        1.0 + 3 * 0.044715 * square
    )
    pre_grad = (slope * act_grad[0].astype(jnp.float32)).astype(jnp.bfloat16)
    grad[0] = lax.dot_general(
        pre_grad, w_in[0], (((1,), (1,)), ((), ())), preferred_element_type=jnp.float32
    ).astype(jnp.bfloat16)


def expert_products(pre, act_grad, w_out, w_in):
    sets, count, _ = pre.shape
    tile = 256

    def moving(width):
        return pl.BlockSpec((1, tile, width), lambda m, i: (m, i, 0))

    def held(weight):
        return pl.BlockSpec((1,) + weight.shape[1:], lambda m, i: (m, 0, 0))

    shape = jax.ShapeDtypeStruct((sets, count, WIDTH), jnp.bfloat16)
    return pl.pallas_call(
        expert_kernel,
        name="expert_products",
        grid=(sets, count // tile),
        out_shape=(shape, shape),
        in_specs=[moving(FF), moving(FF), held(w_out), held(w_in)],
        out_specs=(moving(WIDTH), moving(WIDTH)),
        compiler_params=params(),
        cost_estimate=pl.CostEstimate(
            flops=4 * sets * count * FF * WIDTH,
            bytes_accessed=4 * sets * (count * (FF + WIDTH) + FF * WIDTH),
            transcendentals=sets * count * FF,
        ),
    )(pre, act_grad, w_out, w_in)


def body(
    inputs,
    query_states,
    key_states,
    value_states,
    doc_ids,
    modality,
    expert_ids,
    norm_gain,
    router_w,
    w_in,
    w_out,
    grad_out,
):
    length, width = inputs.shape
    experts = lax.axis_size("seq")
    kept_mask = expert_ids >= 0
    kept_wide = kept_mask.astype(jnp.float32)
    column = modality[:, None] * experts + jnp.where(kept_mask, expert_ids, 0)
    one_hot = (
        column[:, :, None] == jnp.arange(2 * experts, dtype=jnp.int32)[None, None, :]
    ) & kept_mask[:, :, None]
    entries = length * TOP
    flat_hot = one_hot.reshape(entries, 2 * experts).astype(jnp.bfloat16)
    entry_range = jnp.arange(entries, dtype=jnp.int32)
    earlier = (entry_range[:, None] > entry_range[None, :]).astype(jnp.bfloat16)
    before = jnp.dot(earlier, flat_hot, preferred_element_type=jnp.float32)
    slot_rank = jnp.sum(before * flat_hot.astype(jnp.float32), axis=1).astype(jnp.int32)
    slots = jnp.where(kept_mask, column * CAP + slot_rank.reshape(length, TOP), -1)
    slots = jnp.concatenate([slots.T, jnp.full((8 - TOP, length), -1, jnp.int32)], axis=0)

    w_in_local = w_in[:, 0]
    w_out_local = w_out[:, 0]

    got_grads, tokens_grad, table, kv = dispatch_first(
        grad_out, slots, jnp.concatenate([key_states, value_states], axis=1)
    )
    partial_back = product(
        got_grads.reshape(2, experts * CAP, width), w_out_local, True, "back_product"
    )
    act_grad = lax.psum(partial_back, "grp")

    resid_state = attend(query_states, kv.reshape(experts * length, 2 * HEAD_DIM), doc_ids, inputs)
    state_wide = resid_state.astype(jnp.float32)
    scaled = state_wide * norm_gain[None, :]
    raw_part = lax.dot_general(
        router_w,
        scaled.astype(jnp.bfloat16),
        (((0,), (1,)), ((), ())),
        preferred_element_type=jnp.float32,
    )
    square_part = jnp.sum(state_wide * state_wide, axis=1)[None, :]
    stats = small_sum(
        jnp.concatenate([raw_part, square_part, jnp.zeros((7, length), jnp.float32)], axis=0),
        6,
        "sum_stats",
    )
    inv_row = lax.rsqrt(stats[2 * experts] / D + eps_norm)
    inv_rms = inv_row[:, None]
    raw_logits = stats[: 2 * experts].T
    logits = raw_logits * inv_rms
    normed = (scaled * inv_rms).astype(jnp.bfloat16)
    chosen = jnp.sum(jnp.where(one_hot, logits[:, None, :], 0.0), axis=2)
    lifted = jax.nn.sigmoid(chosen)
    denominator = gate_offset + jnp.sum(kept_wide * lifted, axis=1, keepdims=True)
    gates = kept_wide * lifted / denominator
    gates_t = jnp.concatenate([gates.T, jnp.zeros((8 - TOP, length), jnp.float32)], axis=0)

    got_rows = dispatch_next(normed, table)
    partial_value = product(
        got_rows.reshape(2, experts * CAP, width), w_in_local, False, "row_product"
    )
    pre_act = hidden_sum(partial_value.reshape(2 * experts * CAP, FF)).reshape(
        2, experts * CAP, FF
    )
    expert_out, entry_grad = expert_products(pre_act, act_grad, w_out_local, w_in_local)
    mixture, entry_sum, gate_part = collect(
        expert_out.reshape(2, experts, CAP, width),
        entry_grad.reshape(2, experts, CAP, width),
        table,
        gates_t,
        tokens_grad,
    )
    layer_out = (state_wide + mixture).astype(jnp.bfloat16)
    entry_dot = jnp.sum(entry_sum * scaled, axis=1)[None, :]
    row_index = jnp.arange(8, dtype=jnp.int32)[:, None]
    ends = small_sum(jnp.where(row_index == TOP, entry_dot, gate_part), 7, "sum_ends")
    gate_grad = ends[:TOP].T
    gate_dot = jnp.sum(gates * gate_grad, axis=1, keepdims=True)
    logit_grad = kept_wide * (gate_grad - gate_dot) / denominator * lifted * (1.0 - lifted)
    logit_full = jnp.sum(jnp.where(one_hot, logit_grad[:, :, None], 0.0), axis=1)
    router_grad = jnp.dot(
        logit_full, router_w.astype(jnp.float32).T, precision=lax.Precision.HIGHEST
    )
    norm_dot = ends[TOP][:, None] + jnp.sum(logit_full * raw_logits, axis=1, keepdims=True)
    normed_grad = router_grad + entry_sum
    state_grad = (
        grad_out.astype(jnp.float32)
        + inv_rms * norm_gain[None, :] * normed_grad
        - inv_rms**3 / D * state_wide * norm_dot
    )
    return (layer_out, state_grad.astype(jnp.bfloat16))


def solution(mesh):
    in_specs = (
        P("seq", "grp"),
        P("seq", "grp"),
        P("seq", "grp"),
        P("seq", "grp"),
        P(),
        P("seq"),
        P("seq", None),
        P("grp"),
        P("grp", None),
        P(None, "seq", "grp", None),
        P(None, "seq", None, "grp"),
        P("seq", "grp"),
    )
    out_specs = (P("seq", "grp"), P("seq", "grp"))
    return jax.shard_map(body, mesh=mesh, in_specs=in_specs, out_specs=out_specs, check_vma=False)
```

```python
import functools

import jax
import jax.numpy as jnp
from jax import lax
from jax.experimental import pallas as pl
from jax.experimental.pallas import tpu as pltpu
from jax.sharding import PartitionSpec as P

D = 8192
HEADS = 64
KV_HEADS = 8
HEAD_DIM = 128
FF = 1408
TOP = 4
CAP = 16
LEN = 128
WIDTH = 1024

eps_norm = 1e-05
gate_offset = 0.5

MESH = pl.DeviceIdType.MESH
VMEM = pl.BlockSpec(memory_space=pltpu.VMEM)
ANY = pl.BlockSpec(memory_space=pl.ANY)
LIMIT = 56 * 1024 * 1024


def params(collective_id=None):
    if collective_id is None:
        return pltpu.CompilerParams(vmem_limit_bytes=LIMIT)
    return pltpu.CompilerParams(
        collective_id=collective_id, has_side_effects=True, vmem_limit_bytes=LIMIT
    )


class Links:
    def __init__(self, send, recv):
        self.send, self.recv = send, recv
        self.used = 0
        self.started = []

    def ids(self, count):
        first = self.used
        self.used += count
        return [first + i for i in range(count)]

    def copy(self, src, dst, index, axis, peer):
        return pltpu.make_async_remote_copy(
            src_ref=src,
            dst_ref=dst,
            send_sem=self.send.at[index],
            recv_sem=self.recv.at[index],
            device_id={axis: peer},
            device_id_type=MESH,
        )

    def start(self, src, dst, index, axis, peer):
        copy = self.copy(src, dst, index, axis, peer)
        copy.start()
        self.started.append(copy)
        return copy

    def local(self, src, dst, index):
        copy = pltpu.make_async_copy(src, dst, self.send.at[index])
        copy.start()
        return copy

    def finish(self):
        for copy in self.started:
            copy.wait_send()


def greet(axis, peers):
    barrier = pltpu.get_barrier_semaphore()
    for peer in peers:
        pl.semaphore_signal(barrier, inc=1, device_id={axis: peer}, device_id_type=MESH)
    pl.semaphore_wait(barrier, len(peers))


class Flow:
    def __init__(self, which, half):
        me = lax.axis_index("seq")
        y, z, x = me // 8, (me % 8) // 4, me % 4
        self.me, self.z, self.which = me, z, which
        if which == 0:
            self.a, self.b, self.step_a, self.step_b = x, y, 1, 8
        else:
            self.a, self.b, self.step_a, self.step_b = y, x, 8, 1
        self.cols = pl.ds(which * half, half)
        self.home = z * 4 + self.a
        self.zp = self.at(z=1 - z)
        self.ar, self.al = self.at(da=1), self.at(da=3)
        self.br, self.bl = self.at(db=1), self.at(db=3)

    def at(self, z=None, da=0, db=0):
        z = self.z if z is None else z
        return z * 4 + ((self.a + da) % 4) * self.step_a + ((self.b + db) % 4) * self.step_b

    def row(self, db):
        return (self.b + db) % 4

    def block(self, z, da):
        return z * 4 + (self.a + da) % 4

    def codes(self):
        row = lax.broadcasted_iota(jnp.int32, (LEN, LEN), 0)
        owner = (row // 32) * self.step_b + self.z * 4 + self.a * self.step_a
        return (((row // 16) % 2) * 32 + owner) * CAP + row % 16

    def family(self):
        return [self.at(da=d) for d in (1, 2, 3)] + [
            self.at(z=1 - self.z, da=d) for d in (0, 1, 2, 3)
        ]


def near_peers(flow):
    return [flow.zp, flow.ar, flow.al, flow.br, flow.bl]


def all_peers(flow, other):
    return flow.family() + other.family()[:3] + other.family()[4:]


HALF = LEN // 2
SHIFTS = [0, 3, 1, 2]


class GatherStream:
    def __init__(self, links, flow, source, out):
        self.links, self.flow, self.out = links, flow, out
        self.source = source.at[:, flow.cols]
        self.zs = [flow.z, 1 - flow.z]
        self.own_id, self.z_id = links.ids(2)
        self.a1r, self.a1l, self.a2r, self.a2l = (links.ids(2) for _ in range(4))
        self.r_id, self.l_id, self.f_id = (links.ids(8) for _ in range(3))
        self.sent, self.first, self.second, self.far = {}, {}, {}, {}

    def spot(self, order, db=0, rows=None):
        flow = self.flow
        place = flow.at(z=self.zs[order // 4], da=SHIFTS[order % 4], db=db)
        rows = pl.ds(0, LEN) if rows is None else rows
        return self.out.at[place, rows, flow.cols]

    def piece(self, order):
        return self.source if order == 0 else self.spot(order)

    def begin(self):
        self.own = self.links.local(self.source, self.spot(0), self.own_id)
        self.zc = self.links.start(self.source, self.spot(0), self.z_id, "seq", self.flow.zp)
        self.send_a(0)

    def send_a(self, p):
        src, dst = self.piece(p * 4), self.spot(p * 4)
        self.first[p] = (
            self.links.start(src, dst, self.a1r[p], "seq", self.flow.ar),
            self.links.start(src, dst, self.a1l[p], "seq", self.flow.al),
        )

    def forward_a(self, p):
        low, high = pl.ds(0, HALF), pl.ds(HALF, HALF)
        self.first[p][0].wait_recv()
        left = self.spot(p * 4 + 1, rows=low)
        one = self.links.start(left, left, self.a2r[p], "seq", self.flow.ar)
        self.first[p][1].wait_recv()
        right = self.spot(p * 4 + 2, rows=high)
        two = self.links.start(right, right, self.a2l[p], "seq", self.flow.al)
        self.second[p] = (one, two)

    def far_a(self, p):
        self.second[p][0].wait_recv()
        self.second[p][1].wait_recv()

    def other_z(self):
        self.zc.wait_recv()
        self.send_a(1)

    def pick(self, order):
        src, dst = self.piece(order), self.spot(order)
        self.sent[order] = (
            self.links.start(src, dst, self.r_id[order], "seq", self.flow.br),
            self.links.start(src, dst, self.l_id[order], "seq", self.flow.bl),
        )

    def forward_b(self, order):
        right = order % 2 == 0
        self.sent[order][0 if right else 1].wait_recv()
        piece = self.spot(order, db=3 if right else 1)
        self.far[order] = self.links.start(
            piece, piece, self.f_id[order], "seq", self.flow.br if right else self.flow.bl
        )

    def finish(self):
        for order in range(8):
            self.sent[order][1 if order % 2 == 0 else 0].wait_recv()
            self.far[order].wait_recv()
        self.own.wait()


class DispatchStream:
    def __init__(self, links, flow, rows, tokens, table, out_buf, far_buf, got):
        k = flow.which
        self.links, self.flow, self.got = links, flow, got
        self.rows = rows.at[:, flow.cols]
        self.tokens, self.table = tokens.at[k], table.at[k]
        self.out_buf, self.far_buf = out_buf.at[k], far_buf.at[k]
        self.zs = [flow.z, 1 - flow.z]
        (self.z_id,) = links.ids(1)
        self.a1r, self.a1l, self.a2r, self.a2l = (links.ids(2) for _ in range(4))
        self.r_id, self.l_id, self.f1_id, self.f2_id, self.own_id = (
            links.ids(8) for _ in range(5)
        )
        self.sent, self.first, self.second, self.far, self.kept = {}, {}, {}, {}, []
        self.codes = flow.codes()

    def block(self, order):
        return self.flow.block(self.zs[order // 4], SHIFTS[order % 4])

    def begin(self):
        mine = self.tokens.at[self.flow.home]
        self.zc = self.links.start(self.rows, mine, self.z_id, "seq", self.flow.zp)
        self.send_a(0, self.rows)
        self.tokens[self.flow.home] = self.rows[...]

    def send_a(self, p, src=None):
        spot = self.tokens.at[self.block(p * 4)]
        src = spot if src is None else src
        self.first[p] = (
            self.links.start(src, spot, self.a1r[p], "seq", self.flow.ar),
            self.links.start(src, spot, self.a1l[p], "seq", self.flow.al),
        )

    def forward_a(self, p):
        self.first[p][0].wait_recv()
        left = self.tokens.at[self.block(p * 4 + 1), pl.ds(0, HALF)]
        one = self.links.start(left, left, self.a2r[p], "seq", self.flow.ar)
        self.first[p][1].wait_recv()
        right = self.tokens.at[self.block(p * 4 + 2), pl.ds(HALF, HALF)]
        two = self.links.start(right, right, self.a2l[p], "seq", self.flow.al)
        self.second[p] = (one, two)

    def far_a(self, p):
        self.second[p][0].wait_recv()
        self.second[p][1].wait_recv()

    def other_z(self):
        self.zc.wait_recv()
        self.send_a(1)

    def pick(self, order):
        flow, links = self.flow, self.links
        block = self.block(order)
        ids = self.table[block]
        hot = jnp.zeros((LEN, LEN), jnp.float32)
        for k in range(TOP):
            hot = hot + jnp.where(ids[k : k + 1, :] == self.codes, 1.0, 0.0)
        picked = jnp.dot(
            hot.astype(jnp.bfloat16), self.tokens[block], preferred_element_type=jnp.float32
        )
        self.out_buf[:, :, block] = picked.astype(jnp.bfloat16).reshape(4, 2, CAP, WIDTH // 2)
        source = flow.at(z=self.zs[order // 4], da=SHIFTS[order % 4])
        place = self.got.at[:, source, :, flow.cols]
        right = order % 2 == 0
        self.sent[order] = (
            links.start(
                self.out_buf.at[flow.row(2), :, block],
                self.far_buf.at[order],
                self.f1_id[order],
                "seq",
                flow.br if right else flow.bl,
            ),
            links.start(
                self.out_buf.at[flow.row(1), :, block], place, self.r_id[order], "seq", flow.br
            ),
            links.start(
                self.out_buf.at[flow.row(3), :, block], place, self.l_id[order], "seq", flow.bl
            ),
        )
        self.kept.append(
            links.local(self.out_buf.at[flow.b, :, block], place, self.own_id[order])
        )

    def forward_b(self, order):
        flow = self.flow
        right = order % 2 == 0
        self.sent[order][0].wait_recv()
        source = flow.at(
            z=self.zs[order // 4], da=SHIFTS[order % 4], db=3 if right else 1
        )
        self.far[order] = self.links.start(
            self.far_buf.at[order],
            self.got.at[:, source, :, flow.cols],
            self.f2_id[order],
            "seq",
            flow.br if right else flow.bl,
        )

    def finish(self):
        for order in range(8):
            self.sent[order][1].wait_recv()
            self.sent[order][2].wait_recv()
            self.far[order].wait_recv()
        for copy in self.kept:
            copy.wait()


STEPS = [
    ("pick", 0), ("forward_a", 0), ("pick", 1), ("pick", 2), ("other_z",), ("forward_b", 0),
    ("pick", 4), ("far_a", 0), ("pick", 3), ("forward_b", 1), ("forward_b", 2), ("forward_a", 1),
    ("pick", 5), ("pick", 6), ("forward_b", 4), ("forward_b", 3), ("far_a", 1), ("pick", 7),
    ("forward_b", 5), ("forward_b", 6), ("forward_b", 7), ("finish",),
]


def stream_steps(streams):
    def do(name, *given):
        for stream in streams:
            getattr(stream, name)(*given)

    return [functools.partial(do, *step) for step in STEPS]


def tell(links, flow, ids, value, out):
    copies = [
        links.start(value, out.at[flow.home], ids[i], "seq", peer)
        for i, peer in enumerate(flow.family())
    ]
    out[flow.home] = value[...]
    return copies


def first_kernel(
    rows, slots, kv_in, got, tokens, table, kv_out, out_buf, far_buf, send, recv
):
    flows = [Flow(0, WIDTH // 2), Flow(1, WIDTH // 2)]
    kv_flows = [Flow(0, HEAD_DIM), Flow(1, HEAD_DIM)]
    links = Links(send, recv)
    greet("seq", all_peers(*flows))
    gathers = [GatherStream(links, flow, kv_in, kv_out) for flow in kv_flows]
    streams = [
        DispatchStream(links, flow, rows, tokens, table, out_buf, far_buf, got) for flow in flows
    ]
    told = []
    for flow in flows:
        told += tell(links, flow, links.ids(7), slots, table.at[flow.which])
    for stream in gathers + streams:
        stream.begin()
    for copy in told:
        copy.wait_recv()
    for step in stream_steps(gathers + streams):
        step()
    links.finish()


FIRST_SEMS = 2 * 34 + 2 * 49 + 14


def dispatch_first(rows, slots, kv):
    return pl.pallas_call(
        first_kernel,
        name="dispatch_grads",
        out_shape=(
            jax.ShapeDtypeStruct((2, 32, CAP, WIDTH), jnp.bfloat16),
            jax.ShapeDtypeStruct((2, 8, LEN, WIDTH // 2), jnp.bfloat16),
            jax.ShapeDtypeStruct((2, 8, 8, LEN), jnp.int32),
            jax.ShapeDtypeStruct((32, LEN, 2 * HEAD_DIM), jnp.bfloat16),
        ),
        in_specs=[VMEM, VMEM, VMEM],
        out_specs=(ANY, VMEM, VMEM, ANY),
        scratch_shapes=[
            pltpu.VMEM((2, 4, 2, 8, CAP, WIDTH // 2), jnp.bfloat16),
            pltpu.VMEM((2, 8, 2, CAP, WIDTH // 2), jnp.bfloat16),
            pltpu.SemaphoreType.DMA((FIRST_SEMS,)),
            pltpu.SemaphoreType.DMA((FIRST_SEMS,)),
        ],
        compiler_params=params(1),
    )(rows, slots, kv)


DISPATCH_SEMS = 2 * 49


def dispatch_scratch():
    return [
        pltpu.VMEM((2, 4, 2, 8, CAP, WIDTH // 2), jnp.bfloat16),
        pltpu.VMEM((2, 8, 2, CAP, WIDTH // 2), jnp.bfloat16),
    ]


def semaphores(count):
    return [pltpu.SemaphoreType.DMA((count,)), pltpu.SemaphoreType.DMA((count,))]


def share_small(links, part, got):
    me = lax.axis_index("grp")
    copies = [
        links.start(part, got.at[me], i, "grp", (me + 1 + n) % 8)
        for n, i in enumerate(links.ids(7))
    ]
    got[me] = part[...]
    return copies


def add_small(copies, got):
    for copy in copies:
        copy.wait_recv()
    summed = got[0]
    for i in range(1, 8):
        summed = summed + got[i]
    return summed


def greet_both(seq_peers):
    me = lax.axis_index("grp")
    barrier = pltpu.get_barrier_semaphore()
    for peer in seq_peers:
        pl.semaphore_signal(barrier, inc=1, device_id={"seq": peer}, device_id_type=MESH)
    for n in range(1, 8):
        pl.semaphore_signal(
            barrier, inc=1, device_id={"grp": (me + n) % 8}, device_id_type=MESH
        )
    pl.semaphore_wait(barrier, len(seq_peers) + 7)


CHUNK = 32
CHUNKS = 256 // CHUNK
LINE_STEPS = CHUNKS + 12
LINE_SEMS = 8 * CHUNKS


class LineSum:
    def __init__(self, links, part, total, held, sibling, arrived):
        me = lax.axis_index("grp")
        self.links, self.part, self.total = links, part, total
        self.held, self.sibling, self.arrived = held, sibling, arrived
        self.core, chip = me % 2, me // 2
        high = chip // 2
        self.depth = chip + high * (3 - 2 * chip)
        self.twin = chip * 2 + 1 - self.core
        self.inner = me + 2 - 4 * high
        self.outer = (me + 6 + 4 * high) % 8
        self.outgoing, self.incoming = 1 - high, high
        self.pair_id, self.chain_id, self.spread_id, self.share_id = (
            links.ids(2 * CHUNKS)[0] for _ in range(4)
        )

    def local(self, stream, i):
        return pl.ds(pl.multiple_of(stream * 256 + i * CHUNK, CHUNK), CHUNK)

    def whole(self, half, stream, i):
        return pl.ds(pl.multiple_of(half * 512 + stream * 256 + i * CHUNK, CHUNK), CHUNK)

    def pair(self, stream, i):
        return self.links.copy(
            self.part.at[self.whole(1 - self.core, stream, i)],
            self.sibling.at[self.local(stream, i)],
            self.pair_id + stream * CHUNKS + i,
            "grp",
            self.twin,
        )

    def chain(self, stream, i, peer):
        spot = self.local(stream, i)
        return self.links.copy(
            self.held.at[spot],
            self.arrived.at[spot],
            self.chain_id + stream * CHUNKS + i,
            "grp",
            peer,
        )

    def spread(self, stream, i, peer):
        spot = self.total.at[self.whole(self.core, stream, i)]
        return self.links.copy(spot, spot, self.spread_id + stream * CHUNKS + i, "grp", peer)

    def share(self, stream, i):
        spot = self.total.at[self.whole(self.core, stream, i)]
        return self.links.copy(spot, spot, self.share_id + stream * CHUNKS + i, "grp", self.twin)

    def start_pair(self, i):
        if i < CHUNKS:
            self.pair(self.outgoing, i).start()
            self.pair(self.incoming, i).start()

    def begin(self):
        for i in range(4):
            self.start_pair(i)

    def own_sum(self, stream, i):
        self.pair(stream, i).wait_recv()
        return self.part[self.whole(self.core, stream, i)].astype(jnp.float32) + self.sibling[
            self.local(stream, i)
        ].astype(jnp.float32)

    def pass_on(self, stream, i, source, target):
        own = self.own_sum(stream, i)
        spot = self.local(stream, i)
        self.chain(stream, i, source).wait_recv()
        self.held[spot] = (own + self.arrived[spot].astype(jnp.float32)).astype(jnp.bfloat16)
        self.chain(stream, i, target).start()

    def hand_out(self, stream, i, source, target):
        self.spread(stream, i, source).wait_recv()
        self.spread(stream, i, target).start()
        self.share(stream, i).start()

    def step(self, t):
        inner, outer = self.inner, self.outer

        def at(lag):
            return 0 <= t - lag < CHUNKS

        if t < CHUNKS:
            self.start_pair(t + 4)

        @pl.when(self.depth == 0)
        def _():
            if at(0):
                spot = self.local(self.outgoing, t)
                self.held[spot] = self.own_sum(self.outgoing, t).astype(jnp.bfloat16)
                self.chain(self.outgoing, t, inner).start()
            if at(4):
                i = t - 4
                own = self.own_sum(self.incoming, i)
                self.chain(self.incoming, i, inner).wait_recv()
                self.total[self.whole(self.core, self.incoming, i)] = (
                    own + self.arrived[self.local(self.incoming, i)].astype(jnp.float32)
                ).astype(jnp.bfloat16)
                self.spread(self.incoming, i, inner).start()
                self.share(self.incoming, i).start()
            if at(11):
                self.spread(self.outgoing, t - 11, inner).wait_recv()
                self.share(self.outgoing, t - 11).start()

        @pl.when(self.depth == 1)
        def _():
            if at(0):
                self.pass_on(self.outgoing, t, outer, inner)
            if at(2):
                self.pass_on(self.incoming, t - 2, inner, outer)
            if at(6):
                self.hand_out(self.incoming, t - 6, outer, inner)
            if at(9):
                self.hand_out(self.outgoing, t - 9, inner, outer)

    def finish(self):
        @pl.when(self.depth == 0)
        def _():
            for i in range(CHUNKS):
                self.chain(self.outgoing, i, self.inner).wait_send()
                self.spread(self.incoming, i, self.inner).wait_send()

        @pl.when(self.depth == 1)
        def _():
            for i in range(CHUNKS):
                self.chain(self.outgoing, i, self.inner).wait_send()
                self.chain(self.incoming, i, self.outer).wait_send()
                self.spread(self.incoming, i, self.inner).wait_send()
                self.spread(self.outgoing, i, self.outer).wait_send()

        for i in range(CHUNKS):
            for stream in (0, 1):
                self.pair(stream, i).wait_send()
                self.share(stream, i).wait()


def weave(line, steps):
    placed = 0
    for t in range(LINE_STEPS):
        line.step(t)
        due = len(steps) if t == LINE_STEPS - 1 else (t + 1) * len(steps) // LINE_STEPS
        for step in steps[placed:due]:
            step()
        placed = due


def rows_kernel(
    rows, table, part, back_part, got, stats, back_total,
    tokens, out_buf, far_buf, stats_got, held, sibling, arrived, send, recv,
):
    flows = [Flow(0, WIDTH // 2), Flow(1, WIDTH // 2)]
    links = Links(send, recv)
    line = LineSum(links, back_part, back_total, held, sibling, arrived)
    greet_both(near_peers(flows[0]))
    streams = [
        DispatchStream(links, flow, rows, tokens, table, out_buf, far_buf, got) for flow in flows
    ]
    for stream in streams:
        stream.begin()
    copies = share_small(links, part, stats_got)
    line.begin()
    weave(line, stream_steps(streams))
    stats[...] = add_small(copies, stats_got)
    line.finish()
    links.finish()


def dispatch_rows(rows, table, part, back_part):
    return pl.pallas_call(
        rows_kernel,
        name="dispatch_rows",
        out_shape=(
            jax.ShapeDtypeStruct((2, 32, CAP, WIDTH), jnp.bfloat16),
            jax.ShapeDtypeStruct(part.shape, jnp.float32),
            jax.ShapeDtypeStruct(back_part.shape, jnp.bfloat16),
        ),
        in_specs=[VMEM, VMEM, VMEM, VMEM],
        out_specs=(ANY, VMEM, VMEM),
        scratch_shapes=[pltpu.VMEM((2, 8, LEN, WIDTH // 2), jnp.bfloat16)]
        + dispatch_scratch()
        + [pltpu.VMEM((8,) + part.shape, jnp.float32)]
        + [pltpu.VMEM((512, FF), jnp.bfloat16)] * 3
        + semaphores(DISPATCH_SEMS + 7 + LINE_SEMS),
        compiler_params=params(2),
    )(rows, table, part, back_part)


def line_kernel(part, squares, total, square_sum, held, sibling, arrived, small, send, recv):
    links = Links(send, recv)
    line = LineSum(links, part, total, held, sibling, arrived)
    greet_both([])
    line.begin()
    copies = share_small(links, squares, small)
    for t in range(LINE_STEPS):
        line.step(t)
    square_sum[...] = add_small(copies, small)
    line.finish()
    links.finish()


def line_sum(part, squares):
    return pl.pallas_call(
        line_kernel,
        name="line_sum",
        out_shape=(
            jax.ShapeDtypeStruct((1024, FF), jnp.bfloat16),
            jax.ShapeDtypeStruct((8, LEN), jnp.float32),
        ),
        in_specs=[VMEM, VMEM],
        out_specs=(VMEM, VMEM),
        scratch_shapes=[pltpu.VMEM((512, FF), jnp.bfloat16)] * 3
        + [pltpu.VMEM((8, 8, LEN), jnp.float32)]
        + semaphores(LINE_SEMS + 7),
        compiler_params=params(3),
    )(part, squares)


BACK_SHIFTS = [2, 1, 3, 0]


class CollectStream:
    def __init__(self, links, flow, slot, results, scratch, total):
        self.links, self.flow, self.results = links, flow, results
        self.back, self.part, self.far_buf, self.a_half, self.a_full, self.z_buf = (
            ref.at[slot] for ref in scratch
        )
        self.total = total.at[:, flow.cols]
        self.zs = [1 - flow.z, flow.z]
        (self.z_id,) = links.ids(1)
        self.hr, self.hl, self.fr, self.fl = (links.ids(2) for _ in range(4))
        self.r_id, self.l_id, self.f1_id, self.f2_id, self.own_id = (
            links.ids(8) for _ in range(5)
        )
        self.sent, self.far, self.kept, self.halves, self.fulls = {}, {}, {}, {}, {}

    def block(self, order):
        return self.flow.block(self.zs[order // 4], BACK_SHIFTS[order % 4])

    def piece(self, order, db):
        source = self.flow.at(z=self.zs[order // 4], da=BACK_SHIFTS[order % 4], db=db)
        return self.results.at[:, source, :, self.flow.cols]

    def begin(self, order):
        flow, links = self.flow, self.links
        block = self.block(order)
        place = self.back.at[flow.b, :, block]
        right = order % 2 == 0
        self.sent[order] = (
            links.start(
                self.piece(order, 2),
                self.far_buf.at[order],
                self.f1_id[order],
                "seq",
                flow.br if right else flow.bl,
            ),
            links.start(self.piece(order, 1), place, self.r_id[order], "seq", flow.br),
            links.start(self.piece(order, 3), place, self.l_id[order], "seq", flow.bl),
        )
        self.kept[order] = links.local(self.piece(order, 0), place, self.own_id[order])

    def forward_b(self, order):
        flow = self.flow
        right = order % 2 == 0
        self.sent[order][0].wait_recv()
        self.far[order] = self.links.start(
            self.far_buf.at[order],
            self.back.at[flow.row(3 if right else 1), :, self.block(order)],
            self.f2_id[order],
            "seq",
            flow.br if right else flow.bl,
        )

    def arrive(self, order):
        self.kept[order].wait()
        self.sent[order][1].wait_recv()
        self.sent[order][2].wait_recv()
        self.far[order].wait_recv()
        return self.back[:, :, self.block(order)].reshape(LEN, WIDTH // 2)

    def add_on(self, order, summed):
        p, step = order // 4, order % 4
        links, flow = self.links, self.flow
        part = self.part.at[self.block(order)]
        low, high = pl.ds(0, HALF), pl.ds(HALF, HALF)
        if step == 0:
            part[...] = summed.astype(jnp.bfloat16)
            self.halves[p] = (
                links.start(part.at[low], self.a_half.at[p, 0], self.hr[p], "seq", flow.ar),
                links.start(part.at[high], self.a_half.at[p, 1], self.hl[p], "seq", flow.al),
            )
        elif step in (1, 2):
            side = step - 1
            self.halves[p][side].wait_recv()
            arrived = self.a_half[p, side].astype(jnp.float32)
            top, bottom = summed[:HALF], summed[HALF:]
            if side == 0:
                top = top + arrived
            else:
                bottom = bottom + arrived
            part[low] = top.astype(jnp.bfloat16)
            part[high] = bottom.astype(jnp.bfloat16)
            self.fulls[p, side] = links.start(
                part,
                self.a_full.at[p, side],
                (self.fr if side == 0 else self.fl)[p],
                "seq",
                flow.ar if side == 0 else flow.al,
            )
        elif p == 0:
            part[...] = summed.astype(jnp.bfloat16)
        else:
            self.total[...] = summed

    def line_sum(self, p):
        self.fulls[p, 0].wait_recv()
        self.fulls[p, 1].wait_recv()
        return self.a_full[p, 0].astype(jnp.float32) + self.a_full[p, 1].astype(jnp.float32)

    def send_z(self):
        part = self.part.at[self.block(3)]
        part[...] = (part[...].astype(jnp.float32) + self.line_sum(0)).astype(jnp.bfloat16)
        self.zc = self.links.start(part, self.z_buf, self.z_id, "seq", self.flow.zp)

    def finish(self):
        self.total[...] = self.total[...] + self.line_sum(1)
        self.zc.wait_recv()
        self.total[...] = self.total[...] + self.z_buf[...].astype(jnp.float32)


def collect_kernel(
    results, back_results, table, gates, tokens, total, back_total, gate_sum,
    gates_all, back, part, far_buf, a_half, a_full, z_buf, grad_part, grad_got, send, recv,
):
    flows = [Flow(0, WIDTH // 2), Flow(1, WIDTH // 2)]
    links = Links(send, recv)
    greet("seq", all_peers(*flows))
    scratch = (back, part, far_buf, a_half, a_full, z_buf)
    pairs = [
        [
            CollectStream(links, flow, flow.which, results, scratch, total),
            CollectStream(links, flow, 2 + flow.which, back_results, scratch, back_total),
        ]
        for flow in flows
    ]
    streams = [pairs[0][0], pairs[1][0], pairs[0][1], pairs[1][1]]
    told = []
    for flow in flows:
        told += tell(links, flow, links.ids(7), gates, gates_all.at[flow.which])
    turns = [(p * 4 + step, t) for p in (0, 1) for t in (0, 1) for step in range(4)]
    for order, t in turns:
        for pair in pairs:
            pair[t].begin(order)
    for copy in told:
        copy.wait_recv()
    codes = [flow.codes() for flow in flows]
    g_id = [links.ids(8), links.ids(8)]
    grads_sent = []
    mixes = {}

    def mix_of(flow, order):
        k = flow.which
        if (k, order) not in mixes:
            block = pairs[k][0].block(order)
            ids, weight = table[k, block], gates_all[k, block]
            mix = jnp.zeros((LEN, LEN), jnp.float32)
            for c in range(TOP):
                mix = mix + jnp.where(ids[c : c + 1, :] == codes[k], weight[c : c + 1, :], 0.0)
            mixes[k, order] = mix.astype(jnp.bfloat16)
        return mixes[k, order]

    def combine(order, t):
        for flow in flows:
            k = flow.which
            stream = pairs[k][t]
            mix = mix_of(flow, order)
            rows = stream.arrive(order)
            summed = lax.dot_general(
                mix, rows, (((0,), (0,)), ((), ())), preferred_element_type=jnp.float32
            )
            stream.add_on(order, summed)
            if t == 1:
                continue
            block = stream.block(order)
            ids = table[k, block]
            dots = lax.dot_general(
                rows,
                tokens[k, block],
                (((1,), (1,)), ((), ())),
                preferred_element_type=jnp.float32,
            )
            for c in range(TOP):
                grad_part[k, order, c : c + 1, :] = jnp.sum(
                    jnp.where(ids[c : c + 1, :] == codes[k], dots, 0.0), axis=0, keepdims=True
                )
            grad_part[k, order, TOP:, :] = jnp.zeros((8 - TOP, LEN), jnp.float32)
            if order < 7:
                peer = flow.at(z=stream.zs[order // 4], da=BACK_SHIFTS[order % 4])
                grads_sent.append(
                    links.start(
                        grad_part.at[k, order],
                        grad_got.at[k, order],
                        g_id[k][order],
                        "seq",
                        peer,
                    )
                )

    def forward(index):
        if index < len(turns):
            order, t = turns[index]
            for pair in pairs:
                pair[t].forward_b(order)

    forward(0)
    forward(1)
    for index, (order, t) in enumerate(turns):
        forward(index + 2)
        combine(order, t)
        if index in (5, 9):
            for pair in pairs:
                pair[(index - 5) // 4].send_z()
    for stream in streams:
        stream.finish()
    gathered = grad_part[0, 7] + grad_part[1, 7]
    for copy in grads_sent:
        copy.wait_recv()
    for k in range(2):
        for order in range(7):
            gathered = gathered + grad_got[k, order]
    gate_sum[...] = gathered
    links.finish()


COLLECT_SEMS = 4 * 49 + 14 + 16


def collect(results, back_results, table, gates, tokens):
    half = WIDTH // 2
    return pl.pallas_call(
        collect_kernel,
        name="collect",
        out_shape=(
            jax.ShapeDtypeStruct((LEN, WIDTH), jnp.float32),
            jax.ShapeDtypeStruct((LEN, WIDTH), jnp.float32),
            jax.ShapeDtypeStruct((8, LEN), jnp.float32),
        ),
        in_specs=[ANY, ANY, VMEM, VMEM, VMEM],
        out_specs=(VMEM, VMEM, VMEM),
        scratch_shapes=[
            pltpu.VMEM((2, 8, 8, LEN), jnp.float32),
            pltpu.VMEM((4, 4, 2, 8, CAP, half), jnp.bfloat16),
            pltpu.VMEM((4, 8, LEN, half), jnp.bfloat16),
            pltpu.VMEM((4, 8, 2, CAP, half), jnp.bfloat16),
            pltpu.VMEM((4, 2, 2, HALF, half), jnp.bfloat16),
            pltpu.VMEM((4, 2, 2, LEN, half), jnp.bfloat16),
            pltpu.VMEM((4, LEN, half), jnp.bfloat16),
            pltpu.VMEM((2, 8, 8, LEN), jnp.float32),
            pltpu.VMEM((2, 7, 8, LEN), jnp.float32),
            pltpu.SemaphoreType.DMA((COLLECT_SEMS,)),
            pltpu.SemaphoreType.DMA((COLLECT_SEMS,)),
        ],
        compiler_params=params(4),
    )(results, back_results, table, gates, tokens)


def small_sum_kernel(part, total, got, send, recv):
    me = lax.axis_index("grp")
    links = Links(send, recv)
    peers = [(me + shift) % 8 for shift in range(1, 8)]
    ids = links.ids(7)
    greet("grp", peers)
    copies = [
        links.start(part, got.at[me], ids[i], "grp", peers[i]) for i in range(7)
    ]
    got[me] = part[...]
    for copy in copies:
        copy.wait_recv()
    summed = got[0]
    for i in range(1, 8):
        summed = summed + got[i]
    total[...] = summed
    links.finish()


def small_sum(part, collective_id, name):
    shape = part.shape
    return pl.pallas_call(
        small_sum_kernel,
        name=name,
        out_shape=jax.ShapeDtypeStruct(shape, jnp.float32),
        in_specs=[VMEM],
        out_specs=VMEM,
        scratch_shapes=[
            pltpu.VMEM((8,) + shape, jnp.float32),
            pltpu.SemaphoreType.DMA((7,)),
            pltpu.SemaphoreType.DMA((7,)),
        ],
        compiler_params=params(collective_id),
    )(part)


KEYS = 512


def attend_kernel(bounds, query, kv, first_key, query_pos, inputs, resid, best, total, acc):
    scale = HEAD_DIM ** (-0.5) * 1.4426950408889634
    groups = HEADS // KV_HEADS
    best[...] = jnp.full(best.shape, -1e30, jnp.float32)
    total[...] = jnp.zeros(total.shape, jnp.float32)
    acc[...] = jnp.zeros(acc.shape, jnp.float32)

    def step(masked, i, carry):
        start = pl.multiple_of(i * KEYS, KEYS)
        keys = kv[pl.ds(start, KEYS), pl.ds(0, HEAD_DIM)]
        values = kv[pl.ds(start, KEYS), pl.ds(HEAD_DIM, HEAD_DIM)]
        if masked:
            key_pos = start + lax.broadcasted_iota(jnp.int32, (LEN, KEYS), 1)
            allowed = (key_pos <= query_pos[...]) & (key_pos >= first_key[...])
        for h in range(groups):
            scores = lax.dot_general(
                query[:, h * HEAD_DIM : (h + 1) * HEAD_DIM],
                keys,
                (((1,), (1,)), ((), ())),
                preferred_element_type=jnp.float32,
            )
            if masked:
                scores = jnp.where(allowed, scores, -1e30)
            old = best[h]
            new = jnp.maximum(old, jnp.max(scores, axis=1, keepdims=True))
            weights = jnp.exp2((scores - new) * scale)
            shrink = jnp.exp2((old - new) * scale)
            best[h] = new
            total[h] = total[h] * shrink + jnp.sum(weights, axis=1, keepdims=True)
            acc[h] = acc[h] * shrink + jnp.dot(
                weights.astype(jnp.bfloat16), values, preferred_element_type=jnp.float32
            )
        return carry

    lax.fori_loop(bounds[0], bounds[1], functools.partial(step, True), 0)
    lax.fori_loop(bounds[1], bounds[2], functools.partial(step, False), 0)
    lax.fori_loop(bounds[2], bounds[3], functools.partial(step, True), 0)
    for h in range(groups):
        cols = slice(h * HEAD_DIM, (h + 1) * HEAD_DIM)
        attended = (acc[h] / total[h]).astype(jnp.bfloat16).astype(jnp.float32)
        resid[:, cols] = (inputs[:, cols].astype(jnp.float32) + attended).astype(jnp.bfloat16)


def attend(query, kv, doc_ids, inputs):
    first_query = lax.axis_index("seq") * LEN
    query_pos = first_query + jnp.arange(LEN, dtype=jnp.int32)
    query_doc = lax.dynamic_slice_in_dim(doc_ids, first_query, LEN)
    first_key = jnp.sum(
        (doc_ids[None, :] < query_doc[:, None]).astype(jnp.int32), axis=1, keepdims=True
    )
    low = first_key[0, 0] // KEYS
    high = (first_query + LEN + KEYS - 1) // KEYS
    full_low = jnp.minimum((first_key[LEN - 1, 0] + KEYS - 1) // KEYS, high)
    full_high = jnp.maximum((first_query + 1) // KEYS, full_low)
    bounds = jnp.stack([low, full_low, full_high, high])
    groups = HEADS // KV_HEADS
    return pl.pallas_call(
        attend_kernel,
        name="attend",
        out_shape=jax.ShapeDtypeStruct((LEN, WIDTH), jnp.bfloat16),
        in_specs=[pl.BlockSpec(memory_space=pltpu.SMEM)] + [VMEM] * 5,
        out_specs=VMEM,
        scratch_shapes=[
            pltpu.VMEM((groups, LEN, 1), jnp.float32),
            pltpu.VMEM((groups, LEN, 1), jnp.float32),
            pltpu.VMEM((groups, LEN, HEAD_DIM), jnp.float32),
        ],
        compiler_params=params(),
    )(bounds.astype(jnp.int32), query, kv, first_key, query_pos[:, None], inputs)


def product_kernel(turned, rows, weight, out):
    out[0] = lax.dot_general(
        rows[0],
        weight[0],
        (((1,), (1 if turned else 0,)), ((), ())),
        preferred_element_type=jnp.float32,
    ).astype(jnp.bfloat16)


def product(rows, weight, turned, name):
    sets, count, depth = rows.shape
    width = weight.shape[1 if turned else 2]
    return pl.pallas_call(
        functools.partial(product_kernel, turned),
        name=name,
        grid=(sets,),
        out_shape=jax.ShapeDtypeStruct((sets, count, width), jnp.bfloat16),
        in_specs=[
            pl.BlockSpec((1, count, depth), lambda m: (m, 0, 0)),
            pl.BlockSpec((1,) + weight.shape[1:], lambda m: (m, 0, 0)),
        ],
        out_specs=pl.BlockSpec((1, count, width), lambda m: (m, 0, 0)),
        compiler_params=params(),
        cost_estimate=pl.CostEstimate(
            flops=2 * sets * count * depth * width,
            bytes_accessed=2 * sets * (count * depth + depth * width + count * width),
            transcendentals=0,
        ),
    )(rows, weight)


def row_product_kernel(rows, gain, weight, out, squares):
    wide = rows[0].astype(jnp.float32)
    out[0] = jnp.dot(
        (wide * gain[...]).astype(jnp.bfloat16), weight[0], preferred_element_type=jnp.float32
    ).astype(jnp.bfloat16)
    squares[0] = lax.dot_general(
        jnp.ones((8, WIDTH), jnp.float32),
        wide * wide,
        (((1,), (1,)), ((), ())),
        precision=lax.Precision.HIGHEST,
        preferred_element_type=jnp.float32,
    )


def row_product(rows, gain, weight):
    sets, count, depth = rows.shape
    return pl.pallas_call(
        row_product_kernel,
        name="row_product",
        grid=(sets,),
        out_shape=(
            jax.ShapeDtypeStruct((sets, count, FF), jnp.bfloat16),
            jax.ShapeDtypeStruct((sets, 8, count), jnp.float32),
        ),
        in_specs=[
            pl.BlockSpec((1, count, depth), lambda m: (m, 0, 0)),
            pl.BlockSpec((1, depth), lambda m: (0, 0)),
            pl.BlockSpec((1,) + weight.shape[1:], lambda m: (m, 0, 0)),
        ],
        out_specs=(
            pl.BlockSpec((1, count, FF), lambda m: (m, 0, 0)),
            pl.BlockSpec((1, 8, count), lambda m: (m, 0, 0)),
        ),
        compiler_params=params(),
        cost_estimate=pl.CostEstimate(
            flops=2 * sets * count * depth * FF,
            bytes_accessed=2 * sets * (count * depth + depth * FF + count * FF),
            transcendentals=0,
        ),
    )(rows, gain[None, :], weight)


def expert_kernel(pre, inverse, act_grad, w_out, w_in, out, grad):
    root = 0.7978845608028654
    wide = pre[0].astype(jnp.float32) * inverse[0]
    square = wide * wide
    curve = jnp.tanh(root * wide * (1.0 + 0.044715 * square))
    active = (0.5 * wide * (1.0 + curve)).astype(jnp.bfloat16)
    out[0] = jnp.dot(active, w_out[0], preferred_element_type=jnp.float32).astype(jnp.bfloat16)
    slope = 0.5 * (1.0 + curve) + (0.5 * root) * wide * (1.0 - curve * curve) * (
        1.0 + 3 * 0.044715 * square
    )
    pre_grad = (slope * act_grad[0].astype(jnp.float32)).astype(jnp.bfloat16)
    grad[0] = lax.dot_general(
        pre_grad, w_in[0], (((1,), (1,)), ((), ())), preferred_element_type=jnp.float32
    ).astype(jnp.bfloat16)


def expert_products(pre, inverse, act_grad, w_out, w_in):
    sets, count, _ = pre.shape
    tile = 256

    def moving(width):
        return pl.BlockSpec((1, tile, width), lambda m, i: (m, i, 0))

    def held(weight):
        return pl.BlockSpec((1,) + weight.shape[1:], lambda m, i: (m, 0, 0))

    shape = jax.ShapeDtypeStruct((sets, count, WIDTH), jnp.bfloat16)
    return pl.pallas_call(
        expert_kernel,
        name="expert_products",
        grid=(sets, count // tile),
        out_shape=(shape, shape),
        in_specs=[moving(FF), moving(1), moving(FF), held(w_out), held(w_in)],
        out_specs=(moving(WIDTH), moving(WIDTH)),
        compiler_params=params(),
        cost_estimate=pl.CostEstimate(
            flops=4 * sets * count * FF * WIDTH,
            bytes_accessed=4 * sets * (count * (FF + WIDTH) + FF * WIDTH),
            transcendentals=sets * count * FF,
        ),
    )(pre, inverse, act_grad, w_out, w_in)


def body(
    inputs,
    query_states,
    key_states,
    value_states,
    doc_ids,
    modality,
    expert_ids,
    norm_gain,
    router_w,
    w_in,
    w_out,
    grad_out,
):
    length, width = inputs.shape
    experts = lax.axis_size("seq")
    kept_mask = expert_ids >= 0
    kept_wide = kept_mask.astype(jnp.float32)
    column = modality[:, None] * experts + jnp.where(kept_mask, expert_ids, 0)
    one_hot = (
        column[:, :, None] == jnp.arange(2 * experts, dtype=jnp.int32)[None, None, :]
    ) & kept_mask[:, :, None]
    entries = length * TOP
    flat_hot = one_hot.reshape(entries, 2 * experts).astype(jnp.bfloat16)
    entry_range = jnp.arange(entries, dtype=jnp.int32)
    earlier = (entry_range[:, None] > entry_range[None, :]).astype(jnp.bfloat16)
    before = jnp.dot(earlier, flat_hot, preferred_element_type=jnp.float32)
    slot_rank = jnp.sum(before * flat_hot.astype(jnp.float32), axis=1).astype(jnp.int32)
    slots = jnp.where(kept_mask, column * CAP + slot_rank.reshape(length, TOP), -1)
    slots = jnp.concatenate([slots.T, jnp.full((8 - TOP, length), -1, jnp.int32)], axis=0)

    w_in_local = w_in[:, 0]
    w_out_local = w_out[:, 0]

    got_grads, tokens_grad, table, kv = dispatch_first(
        grad_out, slots, jnp.concatenate([key_states, value_states], axis=1)
    )
    entries_all = experts * CAP
    back_part = product(
        got_grads.reshape(2, entries_all, width), w_out_local, True, "back_product"
    )
    resid_state = attend(query_states, kv.reshape(experts * length, 2 * HEAD_DIM), doc_ids, inputs)
    state_wide = resid_state.astype(jnp.float32)
    scaled = state_wide * norm_gain[None, :]
    raw_part = lax.dot_general(
        router_w,
        scaled.astype(jnp.bfloat16),
        (((0,), (1,)), ((), ())),
        preferred_element_type=jnp.float32,
    )
    square_part = jnp.sum(state_wide * state_wide, axis=1)[None, :]
    got_rows, stats, act_grad = dispatch_rows(
        resid_state,
        table,
        jnp.concatenate([raw_part, square_part, jnp.zeros((7, length), jnp.float32)], axis=0),
        back_part.reshape(2 * entries_all, FF),
    )
    inv_row = lax.rsqrt(stats[2 * experts] / D + eps_norm)
    inv_rms = inv_row[:, None]
    raw_logits = stats[: 2 * experts].T
    logits = raw_logits * inv_rms
    chosen = jnp.sum(jnp.where(one_hot, logits[:, None, :], 0.0), axis=2)
    lifted = jax.nn.sigmoid(chosen)
    denominator = gate_offset + jnp.sum(kept_wide * lifted, axis=1, keepdims=True)
    gates = kept_wide * lifted / denominator
    gates_t = jnp.concatenate([gates.T, jnp.zeros((8 - TOP, length), jnp.float32)], axis=0)

    row_part, squares = row_product(
        got_rows.reshape(2, entries_all, width), norm_gain, w_in_local
    )
    pre_act, square_sum = line_sum(
        row_part.reshape(2 * entries_all, FF), squares[:, 0].reshape(8, LEN)
    )
    pre_act = pre_act.reshape(2, entries_all, FF)
    inverse = lax.rsqrt(square_sum / D + eps_norm).reshape(2, entries_all, 1)
    expert_out, entry_grad = expert_products(
        pre_act, inverse, act_grad.reshape(2, entries_all, FF), w_out_local, w_in_local
    )
    mixture, entry_sum, gate_part = collect(
        expert_out.reshape(2, experts, CAP, width),
        entry_grad.reshape(2, experts, CAP, width),
        table,
        gates_t,
        tokens_grad,
    )
    layer_out = (state_wide + mixture).astype(jnp.bfloat16)
    entry_dot = jnp.sum(entry_sum * scaled, axis=1)[None, :]
    row_index = jnp.arange(8, dtype=jnp.int32)[:, None]
    ends = small_sum(jnp.where(row_index == TOP, entry_dot, gate_part), 7, "sum_ends")
    gate_grad = ends[:TOP].T
    gate_dot = jnp.sum(gates * gate_grad, axis=1, keepdims=True)
    logit_grad = kept_wide * (gate_grad - gate_dot) / denominator * lifted * (1.0 - lifted)
    logit_full = jnp.sum(jnp.where(one_hot, logit_grad[:, :, None], 0.0), axis=1)
    router_grad = jnp.dot(
        logit_full, router_w.astype(jnp.float32).T, precision=lax.Precision.HIGHEST
    )
    norm_dot = ends[TOP][:, None] + jnp.sum(logit_full * raw_logits, axis=1, keepdims=True)
    normed_grad = router_grad + entry_sum
    state_grad = (
        grad_out.astype(jnp.float32)
        + inv_rms * norm_gain[None, :] * normed_grad
        - inv_rms**3 / D * state_wide * norm_dot
    )
    return (layer_out, state_grad.astype(jnp.bfloat16))


def solution(mesh):
    in_specs = (
        P("seq", "grp"),
        P("seq", "grp"),
        P("seq", "grp"),
        P("seq", "grp"),
        P(),
        P("seq"),
        P("seq", None),
        P("grp"),
        P("grp", None),
        P(None, "seq", "grp", None),
        P(None, "seq", None, "grp"),
        P("seq", "grp"),
    )
    out_specs = (P("seq", "grp"), P("seq", "grp"))
    return jax.shard_map(body, mesh=mesh, in_specs=in_specs, out_specs=out_specs, check_vma=False)
```

```python
import functools

import jax
import jax.numpy as jnp
from jax import lax
from jax.experimental import pallas as pl
from jax.experimental.pallas import tpu as pltpu
from jax.sharding import PartitionSpec as P

D = 8192
HEADS = 64
KV_HEADS = 8
HEAD_DIM = 128
FF = 1408
TOP = 4
CAP = 16
LEN = 128
WIDTH = 1024

eps_norm = 1e-05
gate_offset = 0.5

MESH = pl.DeviceIdType.MESH
VMEM = pl.BlockSpec(memory_space=pltpu.VMEM)
ANY = pl.BlockSpec(memory_space=pl.ANY)
LIMIT = 56 * 1024 * 1024


def params(collective_id=None):
    if collective_id is None:
        return pltpu.CompilerParams(vmem_limit_bytes=LIMIT)
    return pltpu.CompilerParams(
        collective_id=collective_id, has_side_effects=True, vmem_limit_bytes=LIMIT
    )


class Links:
    def __init__(self, send, recv):
        self.send, self.recv = send, recv
        self.used = 0
        self.started = []

    def ids(self, count):
        first = self.used
        self.used += count
        return [first + i for i in range(count)]

    def copy(self, src, dst, index, axis, peer):
        return pltpu.make_async_remote_copy(
            src_ref=src,
            dst_ref=dst,
            send_sem=self.send.at[index],
            recv_sem=self.recv.at[index],
            device_id={axis: peer},
            device_id_type=MESH,
        )

    def start(self, src, dst, index, axis, peer):
        copy = self.copy(src, dst, index, axis, peer)
        copy.start()
        self.started.append(copy)
        return copy

    def local(self, src, dst, index):
        copy = pltpu.make_async_copy(src, dst, self.send.at[index])
        copy.start()
        return copy

    def finish(self):
        for copy in self.started:
            copy.wait_send()


def greet(axis, peers):
    barrier = pltpu.get_barrier_semaphore()
    for peer in peers:
        pl.semaphore_signal(barrier, inc=1, device_id={axis: peer}, device_id_type=MESH)
    pl.semaphore_wait(barrier, len(peers))


class Flow:
    def __init__(self, which, half):
        me = lax.axis_index("seq")
        y, z, x = me // 8, (me % 8) // 4, me % 4
        self.me, self.z, self.which = me, z, which
        if which == 0:
            self.a, self.b, self.step_a, self.step_b = x, y, 1, 8
        else:
            self.a, self.b, self.step_a, self.step_b = y, x, 8, 1
        self.cols = pl.ds(which * half, half)
        self.home = z * 4 + self.a
        self.zp = self.at(z=1 - z)
        self.ar, self.al = self.at(da=1), self.at(da=3)
        self.br, self.bl = self.at(db=1), self.at(db=3)

    def at(self, z=None, da=0, db=0):
        z = self.z if z is None else z
        return z * 4 + ((self.a + da) % 4) * self.step_a + ((self.b + db) % 4) * self.step_b

    def row(self, db):
        return (self.b + db) % 4

    def block(self, z, da):
        return z * 4 + (self.a + da) % 4

    def codes(self):
        row = lax.broadcasted_iota(jnp.int32, (LEN, LEN), 0)
        owner = (row // 32) * self.step_b + self.z * 4 + self.a * self.step_a
        return (((row // 16) % 2) * 32 + owner) * CAP + row % 16

    def family(self):
        return [self.at(da=d) for d in (1, 2, 3)] + [
            self.at(z=1 - self.z, da=d) for d in (0, 1, 2, 3)
        ]


def near_peers(flow):
    return [flow.zp, flow.ar, flow.al, flow.br, flow.bl]


def all_peers(flow, other):
    return flow.family() + other.family()[:3] + other.family()[4:]


HALF = LEN // 2
SHIFTS = [0, 3, 1, 2]


class GatherStream:
    def __init__(self, links, flow, source, out):
        self.links, self.flow, self.out = links, flow, out
        self.source = source.at[:, flow.cols]
        self.zs = [flow.z, 1 - flow.z]
        self.own_id, self.z_id = links.ids(2)
        self.a1r, self.a1l, self.a2r, self.a2l = (links.ids(2) for _ in range(4))
        self.r_id, self.l_id, self.f_id = (links.ids(8) for _ in range(3))
        self.sent, self.first, self.second, self.far = {}, {}, {}, {}

    def spot(self, order, db=0, rows=None):
        flow = self.flow
        place = flow.at(z=self.zs[order // 4], da=SHIFTS[order % 4], db=db)
        rows = pl.ds(0, LEN) if rows is None else rows
        return self.out.at[place, rows, flow.cols]

    def piece(self, order):
        return self.source if order == 0 else self.spot(order)

    def begin(self):
        self.own = self.links.local(self.source, self.spot(0), self.own_id)
        self.zc = self.links.start(self.source, self.spot(0), self.z_id, "seq", self.flow.zp)
        self.send_a(0)

    def send_a(self, p):
        src, dst = self.piece(p * 4), self.spot(p * 4)
        self.first[p] = (
            self.links.start(src, dst, self.a1r[p], "seq", self.flow.ar),
            self.links.start(src, dst, self.a1l[p], "seq", self.flow.al),
        )

    def forward_a(self, p):
        low, high = pl.ds(0, HALF), pl.ds(HALF, HALF)
        self.first[p][0].wait_recv()
        left = self.spot(p * 4 + 1, rows=low)
        one = self.links.start(left, left, self.a2r[p], "seq", self.flow.ar)
        self.first[p][1].wait_recv()
        right = self.spot(p * 4 + 2, rows=high)
        two = self.links.start(right, right, self.a2l[p], "seq", self.flow.al)
        self.second[p] = (one, two)

    def far_a(self, p):
        self.second[p][0].wait_recv()
        self.second[p][1].wait_recv()

    def other_z(self):
        self.zc.wait_recv()
        self.send_a(1)

    def pick(self, order):
        src, dst = self.piece(order), self.spot(order)
        self.sent[order] = (
            self.links.start(src, dst, self.r_id[order], "seq", self.flow.br),
            self.links.start(src, dst, self.l_id[order], "seq", self.flow.bl),
        )

    def forward_b(self, order):
        right = order % 2 == 0
        self.sent[order][0 if right else 1].wait_recv()
        piece = self.spot(order, db=3 if right else 1)
        self.far[order] = self.links.start(
            piece, piece, self.f_id[order], "seq", self.flow.br if right else self.flow.bl
        )

    def finish(self):
        for order in range(8):
            self.sent[order][1 if order % 2 == 0 else 0].wait_recv()
            self.far[order].wait_recv()
        self.own.wait()


class DispatchStream:
    def __init__(self, links, flow, rows, tokens, table, out_buf, far_buf, got):
        k = flow.which
        self.links, self.flow, self.got = links, flow, got
        self.rows = rows.at[:, flow.cols]
        self.tokens, self.table = tokens.at[k], table.at[k]
        self.out_buf, self.far_buf = out_buf.at[k], far_buf.at[k]
        self.zs = [flow.z, 1 - flow.z]
        (self.z_id,) = links.ids(1)
        self.a1r, self.a1l, self.a2r, self.a2l = (links.ids(2) for _ in range(4))
        self.r_id, self.l_id, self.f1_id, self.f2_id, self.own_id = (
            links.ids(8) for _ in range(5)
        )
        self.sent, self.first, self.second, self.far, self.kept = {}, {}, {}, {}, []
        self.codes = flow.codes()

    def block(self, order):
        return self.flow.block(self.zs[order // 4], SHIFTS[order % 4])

    def begin(self):
        mine = self.tokens.at[self.flow.home]
        self.zc = self.links.start(self.rows, mine, self.z_id, "seq", self.flow.zp)
        self.send_a(0, self.rows)
        self.tokens[self.flow.home] = self.rows[...]

    def send_a(self, p, src=None):
        spot = self.tokens.at[self.block(p * 4)]
        src = spot if src is None else src
        self.first[p] = (
            self.links.start(src, spot, self.a1r[p], "seq", self.flow.ar),
            self.links.start(src, spot, self.a1l[p], "seq", self.flow.al),
        )

    def forward_a(self, p):
        self.first[p][0].wait_recv()
        left = self.tokens.at[self.block(p * 4 + 1), pl.ds(0, HALF)]
        one = self.links.start(left, left, self.a2r[p], "seq", self.flow.ar)
        self.first[p][1].wait_recv()
        right = self.tokens.at[self.block(p * 4 + 2), pl.ds(HALF, HALF)]
        two = self.links.start(right, right, self.a2l[p], "seq", self.flow.al)
        self.second[p] = (one, two)

    def far_a(self, p):
        self.second[p][0].wait_recv()
        self.second[p][1].wait_recv()

    def other_z(self):
        self.zc.wait_recv()
        self.send_a(1)

    def pick(self, order):
        flow, links = self.flow, self.links
        block = self.block(order)
        ids = self.table[block]
        hot = jnp.zeros((LEN, LEN), jnp.float32)
        for k in range(TOP):
            hot = hot + jnp.where(ids[k : k + 1, :] == self.codes, 1.0, 0.0)
        picked = jnp.dot(
            hot.astype(jnp.bfloat16), self.tokens[block], preferred_element_type=jnp.float32
        )
        self.out_buf[:, :, block] = picked.astype(jnp.bfloat16).reshape(4, 2, CAP, WIDTH // 2)
        source = flow.at(z=self.zs[order // 4], da=SHIFTS[order % 4])
        place = self.got.at[:, source, :, flow.cols]
        right = order % 2 == 0
        self.sent[order] = (
            links.start(
                self.out_buf.at[flow.row(2), :, block],
                self.far_buf.at[order],
                self.f1_id[order],
                "seq",
                flow.br if right else flow.bl,
            ),
            links.start(
                self.out_buf.at[flow.row(1), :, block], place, self.r_id[order], "seq", flow.br
            ),
            links.start(
                self.out_buf.at[flow.row(3), :, block], place, self.l_id[order], "seq", flow.bl
            ),
        )
        self.kept.append(
            links.local(self.out_buf.at[flow.b, :, block], place, self.own_id[order])
        )

    def forward_b(self, order):
        flow = self.flow
        right = order % 2 == 0
        self.sent[order][0].wait_recv()
        source = flow.at(
            z=self.zs[order // 4], da=SHIFTS[order % 4], db=3 if right else 1
        )
        self.far[order] = self.links.start(
            self.far_buf.at[order],
            self.got.at[:, source, :, flow.cols],
            self.f2_id[order],
            "seq",
            flow.br if right else flow.bl,
        )

    def finish(self):
        for order in range(8):
            self.sent[order][1].wait_recv()
            self.sent[order][2].wait_recv()
            self.far[order].wait_recv()
        for copy in self.kept:
            copy.wait()


STEPS = [
    ("pick", 0), ("forward_a", 0), ("pick", 1), ("pick", 2), ("other_z",), ("forward_b", 0),
    ("pick", 4), ("far_a", 0), ("pick", 3), ("forward_b", 1), ("forward_b", 2), ("forward_a", 1),
    ("pick", 5), ("pick", 6), ("forward_b", 4), ("forward_b", 3), ("far_a", 1), ("pick", 7),
    ("forward_b", 5), ("forward_b", 6), ("forward_b", 7), ("finish",),
]


def stream_steps(streams):
    def do(name, *given):
        for stream in streams:
            getattr(stream, name)(*given)

    return [functools.partial(do, *step) for step in STEPS]


def tell(links, flow, ids, value, out):
    copies = [
        links.start(value, out.at[flow.home], ids[i], "seq", peer)
        for i, peer in enumerate(flow.family())
    ]
    out[flow.home] = value[...]
    return copies


def first_kernel(
    rows, slots, kv_in, got, tokens, table, kv_out, out_buf, far_buf, send, recv
):
    flows = [Flow(0, WIDTH // 2), Flow(1, WIDTH // 2)]
    kv_flows = [Flow(0, HEAD_DIM), Flow(1, HEAD_DIM)]
    links = Links(send, recv)
    greet("seq", all_peers(*flows))
    gathers = [GatherStream(links, flow, kv_in, kv_out) for flow in kv_flows]
    streams = [
        DispatchStream(links, flow, rows, tokens, table, out_buf, far_buf, got) for flow in flows
    ]
    told = []
    for flow in flows:
        told += tell(links, flow, links.ids(7), slots, table.at[flow.which])
    for stream in gathers + streams:
        stream.begin()
    for copy in told:
        copy.wait_recv()
    for step in stream_steps(gathers + streams):
        step()
    links.finish()


FIRST_SEMS = 2 * 34 + 2 * 49 + 14


def dispatch_first(rows, slots, kv):
    return pl.pallas_call(
        first_kernel,
        name="dispatch_grads",
        out_shape=(
            jax.ShapeDtypeStruct((2, 32, CAP, WIDTH), jnp.bfloat16),
            jax.ShapeDtypeStruct((2, 8, LEN, WIDTH // 2), jnp.bfloat16),
            jax.ShapeDtypeStruct((2, 8, 8, LEN), jnp.int32),
            jax.ShapeDtypeStruct((32, LEN, 2 * HEAD_DIM), jnp.bfloat16),
        ),
        in_specs=[VMEM, VMEM, VMEM],
        out_specs=(ANY, VMEM, VMEM, ANY),
        scratch_shapes=[
            pltpu.VMEM((2, 4, 2, 8, CAP, WIDTH // 2), jnp.bfloat16),
            pltpu.VMEM((2, 8, 2, CAP, WIDTH // 2), jnp.bfloat16),
            pltpu.SemaphoreType.DMA((FIRST_SEMS,)),
            pltpu.SemaphoreType.DMA((FIRST_SEMS,)),
        ],
        compiler_params=params(1),
    )(rows, slots, kv)


DISPATCH_SEMS = 2 * 49


def dispatch_scratch():
    return [
        pltpu.VMEM((2, 4, 2, 8, CAP, WIDTH // 2), jnp.bfloat16),
        pltpu.VMEM((2, 8, 2, CAP, WIDTH // 2), jnp.bfloat16),
    ]


def semaphores(count):
    return [pltpu.SemaphoreType.DMA((count,)), pltpu.SemaphoreType.DMA((count,))]


def share_small(links, part, got):
    me = lax.axis_index("grp")
    copies = [
        links.start(part, got.at[me], i, "grp", (me + 1 + n) % 8)
        for n, i in enumerate(links.ids(7))
    ]
    got[me] = part[...]
    return copies


def add_small(copies, got):
    for copy in copies:
        copy.wait_recv()
    summed = got[0]
    for i in range(1, 8):
        summed = summed + got[i]
    return summed


def greet_both(seq_peers):
    me = lax.axis_index("grp")
    barrier = pltpu.get_barrier_semaphore()
    for peer in seq_peers:
        pl.semaphore_signal(barrier, inc=1, device_id={"seq": peer}, device_id_type=MESH)
    for n in range(1, 8):
        pl.semaphore_signal(
            barrier, inc=1, device_id={"grp": (me + n) % 8}, device_id_type=MESH
        )
    pl.semaphore_wait(barrier, len(seq_peers) + 7)


CHUNK = 32
CHUNKS = 256 // CHUNK
LINE_STEPS = CHUNKS + 13
CLOSE_LAGS = (0, 2, 4, 6, 9, 11)
WIDE_LAGS = (2, 4, 6, 8, 10, 12)
LINE_SEMS = 8 * CHUNKS


class LineSum:
    def __init__(self, links, part, total, held, sibling, arrived, lags):
        me = lax.axis_index("grp")
        self.lags = lags
        self.links, self.part, self.total = links, part, total
        self.held, self.sibling, self.arrived = held, sibling, arrived
        self.core, chip = me % 2, me // 2
        high = chip // 2
        self.depth = chip + high * (3 - 2 * chip)
        self.twin = chip * 2 + 1 - self.core
        self.inner = me + 2 - 4 * high
        self.outer = (me + 6 + 4 * high) % 8
        self.outgoing, self.incoming = 1 - high, high
        self.pair_id, self.chain_id, self.spread_id, self.share_id = (
            links.ids(2 * CHUNKS)[0] for _ in range(4)
        )

    def local(self, stream, i):
        return pl.ds(pl.multiple_of(stream * 256 + i * CHUNK, CHUNK), CHUNK)

    def whole(self, half, stream, i):
        return pl.ds(pl.multiple_of(half * 512 + stream * 256 + i * CHUNK, CHUNK), CHUNK)

    def pair(self, stream, i):
        return self.links.copy(
            self.part.at[self.whole(1 - self.core, stream, i)],
            self.sibling.at[self.local(stream, i)],
            self.pair_id + stream * CHUNKS + i,
            "grp",
            self.twin,
        )

    def chain(self, stream, i, peer):
        spot = self.local(stream, i)
        return self.links.copy(
            self.held.at[spot],
            self.arrived.at[spot],
            self.chain_id + stream * CHUNKS + i,
            "grp",
            peer,
        )

    def spread(self, stream, i, peer):
        spot = self.total.at[self.whole(self.core, stream, i)]
        return self.links.copy(spot, spot, self.spread_id + stream * CHUNKS + i, "grp", peer)

    def share(self, stream, i):
        spot = self.total.at[self.whole(self.core, stream, i)]
        return self.links.copy(spot, spot, self.share_id + stream * CHUNKS + i, "grp", self.twin)

    def start_pair(self, i):
        if i < CHUNKS:
            self.pair(self.outgoing, i).start()
            self.pair(self.incoming, i).start()

    def begin(self):
        for i in range(4):
            self.start_pair(i)

    def own_sum(self, stream, i):
        self.pair(stream, i).wait_recv()
        return self.part[self.whole(self.core, stream, i)].astype(jnp.float32) + self.sibling[
            self.local(stream, i)
        ].astype(jnp.float32)

    def pass_on(self, stream, i, source, target):
        own = self.own_sum(stream, i)
        spot = self.local(stream, i)
        self.chain(stream, i, source).wait_recv()
        self.held[spot] = (own + self.arrived[spot].astype(jnp.float32)).astype(jnp.bfloat16)
        self.chain(stream, i, target).start()

    def hand_out(self, stream, i, source, target):
        self.spread(stream, i, source).wait_recv()
        self.spread(stream, i, target).start()
        self.share(stream, i).start()

    def step(self, t):
        inner, outer = self.inner, self.outer
        pass_out, pass_in, end, hand_in, hand_back, last = self.lags

        def at(lag):
            return 0 <= t - lag < CHUNKS

        if t < CHUNKS:
            self.start_pair(t + 4)

        @pl.when(self.depth == 0)
        def _():
            if at(0):
                spot = self.local(self.outgoing, t)
                self.held[spot] = self.own_sum(self.outgoing, t).astype(jnp.bfloat16)
                self.chain(self.outgoing, t, inner).start()
            if at(end):
                i = t - end
                own = self.own_sum(self.incoming, i)
                self.chain(self.incoming, i, inner).wait_recv()
                self.total[self.whole(self.core, self.incoming, i)] = (
                    own + self.arrived[self.local(self.incoming, i)].astype(jnp.float32)
                ).astype(jnp.bfloat16)
                self.spread(self.incoming, i, inner).start()
                self.share(self.incoming, i).start()
            if at(last):
                self.spread(self.outgoing, t - last, inner).wait_recv()
                self.share(self.outgoing, t - last).start()

        @pl.when(self.depth == 1)
        def _():
            if at(pass_out):
                self.pass_on(self.outgoing, t - pass_out, outer, inner)
            if at(pass_in):
                self.pass_on(self.incoming, t - pass_in, inner, outer)
            if at(hand_in):
                self.hand_out(self.incoming, t - hand_in, outer, inner)
            if at(hand_back):
                self.hand_out(self.outgoing, t - hand_back, inner, outer)

    def finish(self):
        @pl.when(self.depth == 0)
        def _():
            for i in range(CHUNKS):
                self.chain(self.outgoing, i, self.inner).wait_send()
                self.spread(self.incoming, i, self.inner).wait_send()

        @pl.when(self.depth == 1)
        def _():
            for i in range(CHUNKS):
                self.chain(self.outgoing, i, self.inner).wait_send()
                self.chain(self.incoming, i, self.outer).wait_send()
                self.spread(self.incoming, i, self.inner).wait_send()
                self.spread(self.outgoing, i, self.outer).wait_send()

        for i in range(CHUNKS):
            for stream in (0, 1):
                self.pair(stream, i).wait_send()
                self.share(stream, i).wait()


def weave(line, steps):
    placed = 0
    for t in range(LINE_STEPS):
        line.step(t)
        due = len(steps) if t == LINE_STEPS - 1 else (t + 1) * len(steps) // LINE_STEPS
        for step in steps[placed:due]:
            step()
        placed = due


def rows_kernel(
    rows, table, part, back_part, got, stats, back_total,
    tokens, out_buf, far_buf, stats_got, held, sibling, arrived, send, recv,
):
    flows = [Flow(0, WIDTH // 2), Flow(1, WIDTH // 2)]
    links = Links(send, recv)
    line = LineSum(links, back_part, back_total, held, sibling, arrived, WIDE_LAGS)
    greet_both(near_peers(flows[0]))
    streams = [
        DispatchStream(links, flow, rows, tokens, table, out_buf, far_buf, got) for flow in flows
    ]
    for stream in streams:
        stream.begin()
    copies = share_small(links, part, stats_got)
    line.begin()
    weave(line, stream_steps(streams))
    stats[...] = add_small(copies, stats_got)
    line.finish()
    links.finish()


def dispatch_rows(rows, table, part, back_part):
    return pl.pallas_call(
        rows_kernel,
        name="dispatch_rows",
        out_shape=(
            jax.ShapeDtypeStruct((2, 32, CAP, WIDTH), jnp.bfloat16),
            jax.ShapeDtypeStruct(part.shape, jnp.float32),
            jax.ShapeDtypeStruct(back_part.shape, jnp.bfloat16),
        ),
        in_specs=[VMEM, VMEM, VMEM, VMEM],
        out_specs=(ANY, VMEM, VMEM),
        scratch_shapes=[pltpu.VMEM((2, 8, LEN, WIDTH // 2), jnp.bfloat16)]
        + dispatch_scratch()
        + [pltpu.VMEM((8,) + part.shape, jnp.float32)]
        + [pltpu.VMEM((512, FF), jnp.bfloat16)] * 3
        + semaphores(DISPATCH_SEMS + 7 + LINE_SEMS),
        compiler_params=params(2),
    )(rows, table, part, back_part)


def line_kernel(part, squares, total, square_sum, held, sibling, arrived, small, send, recv):
    links = Links(send, recv)
    line = LineSum(links, part, total, held, sibling, arrived, CLOSE_LAGS)
    greet_both([])
    line.begin()
    copies = share_small(links, squares, small)
    for t in range(LINE_STEPS):
        line.step(t)
    square_sum[...] = add_small(copies, small)
    line.finish()
    links.finish()


def line_sum(part, squares):
    return pl.pallas_call(
        line_kernel,
        name="line_sum",
        out_shape=(
            jax.ShapeDtypeStruct((1024, FF), jnp.bfloat16),
            jax.ShapeDtypeStruct((8, LEN), jnp.float32),
        ),
        in_specs=[VMEM, VMEM],
        out_specs=(VMEM, VMEM),
        scratch_shapes=[pltpu.VMEM((512, FF), jnp.bfloat16)] * 3
        + [pltpu.VMEM((8, 8, LEN), jnp.float32)]
        + semaphores(LINE_SEMS + 7),
        compiler_params=params(3),
    )(part, squares)


BACK_SHIFTS = [2, 1, 3, 0]


class CollectStream:
    def __init__(self, links, flow, slot, results, scratch, total):
        self.links, self.flow, self.results = links, flow, results
        self.back, self.part, self.far_buf, self.a_half, self.a_full, self.z_buf = (
            ref.at[slot] for ref in scratch
        )
        self.total = total.at[:, flow.cols]
        self.zs = [1 - flow.z, flow.z]
        (self.z_id,) = links.ids(1)
        self.hr, self.hl, self.fr, self.fl = (links.ids(2) for _ in range(4))
        self.r_id, self.l_id, self.f1_id, self.f2_id, self.own_id = (
            links.ids(8) for _ in range(5)
        )
        self.sent, self.far, self.kept, self.halves, self.fulls = {}, {}, {}, {}, {}

    def block(self, order):
        return self.flow.block(self.zs[order // 4], BACK_SHIFTS[order % 4])

    def piece(self, order, db):
        source = self.flow.at(z=self.zs[order // 4], da=BACK_SHIFTS[order % 4], db=db)
        return self.results.at[:, source, :, self.flow.cols]

    def begin(self, order):
        flow, links = self.flow, self.links
        block = self.block(order)
        place = self.back.at[flow.b, :, block]
        right = order % 2 == 0
        self.sent[order] = (
            links.start(
                self.piece(order, 2),
                self.far_buf.at[order],
                self.f1_id[order],
                "seq",
                flow.br if right else flow.bl,
            ),
            links.start(self.piece(order, 1), place, self.r_id[order], "seq", flow.br),
            links.start(self.piece(order, 3), place, self.l_id[order], "seq", flow.bl),
        )
        self.kept[order] = links.local(self.piece(order, 0), place, self.own_id[order])

    def forward_b(self, order):
        flow = self.flow
        right = order % 2 == 0
        self.sent[order][0].wait_recv()
        self.far[order] = self.links.start(
            self.far_buf.at[order],
            self.back.at[flow.row(3 if right else 1), :, self.block(order)],
            self.f2_id[order],
            "seq",
            flow.br if right else flow.bl,
        )

    def arrive(self, order):
        self.kept[order].wait()
        self.sent[order][1].wait_recv()
        self.sent[order][2].wait_recv()
        self.far[order].wait_recv()
        return self.back[:, :, self.block(order)].reshape(LEN, WIDTH // 2)

    def add_on(self, order, summed):
        p, step = order // 4, order % 4
        links, flow = self.links, self.flow
        part = self.part.at[self.block(order)]
        low, high = pl.ds(0, HALF), pl.ds(HALF, HALF)
        if step == 0:
            part[...] = summed.astype(jnp.bfloat16)
            self.halves[p] = (
                links.start(part.at[low], self.a_half.at[p, 0], self.hr[p], "seq", flow.ar),
                links.start(part.at[high], self.a_half.at[p, 1], self.hl[p], "seq", flow.al),
            )
        elif step in (1, 2):
            side = step - 1
            self.halves[p][side].wait_recv()
            arrived = self.a_half[p, side].astype(jnp.float32)
            top, bottom = summed[:HALF], summed[HALF:]
            if side == 0:
                top = top + arrived
            else:
                bottom = bottom + arrived
            part[low] = top.astype(jnp.bfloat16)
            part[high] = bottom.astype(jnp.bfloat16)
            self.fulls[p, side] = links.start(
                part,
                self.a_full.at[p, side],
                (self.fr if side == 0 else self.fl)[p],
                "seq",
                flow.ar if side == 0 else flow.al,
            )
        elif p == 0:
            part[...] = summed.astype(jnp.bfloat16)
        else:
            self.total[...] = summed

    def line_sum(self, p):
        self.fulls[p, 0].wait_recv()
        self.fulls[p, 1].wait_recv()
        return self.a_full[p, 0].astype(jnp.float32) + self.a_full[p, 1].astype(jnp.float32)

    def send_z(self):
        part = self.part.at[self.block(3)]
        part[...] = (part[...].astype(jnp.float32) + self.line_sum(0)).astype(jnp.bfloat16)
        self.zc = self.links.start(part, self.z_buf, self.z_id, "seq", self.flow.zp)

    def finish(self):
        self.total[...] = self.total[...] + self.line_sum(1)
        self.zc.wait_recv()
        self.total[...] = self.total[...] + self.z_buf[...].astype(jnp.float32)


def collect_kernel(
    results, back_results, table, gates, tokens, total, back_total, gate_sum,
    gates_all, back, part, far_buf, a_half, a_full, z_buf, grad_part, grad_got, send, recv,
):
    flows = [Flow(0, WIDTH // 2), Flow(1, WIDTH // 2)]
    links = Links(send, recv)
    greet("seq", all_peers(*flows))
    scratch = (back, part, far_buf, a_half, a_full, z_buf)
    pairs = [
        [
            CollectStream(links, flow, flow.which, results, scratch, total),
            CollectStream(links, flow, 2 + flow.which, back_results, scratch, back_total),
        ]
        for flow in flows
    ]
    streams = [pairs[0][0], pairs[1][0], pairs[0][1], pairs[1][1]]
    told = []
    for flow in flows:
        told += tell(links, flow, links.ids(7), gates, gates_all.at[flow.which])
    turns = [(p * 4 + step, t) for p in (0, 1) for t in (0, 1) for step in range(4)]
    for order, t in turns:
        for pair in pairs:
            pair[t].begin(order)
    for copy in told:
        copy.wait_recv()
    codes = [flow.codes() for flow in flows]
    g_id = [links.ids(8), links.ids(8)]
    grads_sent = []
    mixes = {}

    def mix_of(flow, order):
        k = flow.which
        if (k, order) not in mixes:
            block = pairs[k][0].block(order)
            ids, weight = table[k, block], gates_all[k, block]
            mix = jnp.zeros((LEN, LEN), jnp.float32)
            for c in range(TOP):
                mix = mix + jnp.where(ids[c : c + 1, :] == codes[k], weight[c : c + 1, :], 0.0)
            mixes[k, order] = mix.astype(jnp.bfloat16)
        return mixes[k, order]

    def combine(order, t):
        for flow in flows:
            k = flow.which
            stream = pairs[k][t]
            mix = mix_of(flow, order)
            rows = stream.arrive(order)
            summed = lax.dot_general(
                mix, rows, (((0,), (0,)), ((), ())), preferred_element_type=jnp.float32
            )
            stream.add_on(order, summed)
            if t == 1:
                continue
            block = stream.block(order)
            ids = table[k, block]
            dots = lax.dot_general(
                rows,
                tokens[k, block],
                (((1,), (1,)), ((), ())),
                preferred_element_type=jnp.float32,
            )
            for c in range(TOP):
                grad_part[k, order, c : c + 1, :] = jnp.sum(
                    jnp.where(ids[c : c + 1, :] == codes[k], dots, 0.0), axis=0, keepdims=True
                )
            grad_part[k, order, TOP:, :] = jnp.zeros((8 - TOP, LEN), jnp.float32)
            if order < 7:
                peer = flow.at(z=stream.zs[order // 4], da=BACK_SHIFTS[order % 4])
                grads_sent.append(
                    links.start(
                        grad_part.at[k, order],
                        grad_got.at[k, order],
                        g_id[k][order],
                        "seq",
                        peer,
                    )
                )

    def forward(index):
        if index < len(turns):
            order, t = turns[index]
            for pair in pairs:
                pair[t].forward_b(order)

    forward(0)
    forward(1)
    for index, (order, t) in enumerate(turns):
        forward(index + 2)
        combine(order, t)
        if index in (5, 9):
            for pair in pairs:
                pair[(index - 5) // 4].send_z()
    for stream in streams:
        stream.finish()
    gathered = grad_part[0, 7] + grad_part[1, 7]
    for copy in grads_sent:
        copy.wait_recv()
    for k in range(2):
        for order in range(7):
            gathered = gathered + grad_got[k, order]
    gate_sum[...] = gathered
    links.finish()


COLLECT_SEMS = 4 * 49 + 14 + 16


def collect(results, back_results, table, gates, tokens):
    half = WIDTH // 2
    return pl.pallas_call(
        collect_kernel,
        name="collect",
        out_shape=(
            jax.ShapeDtypeStruct((LEN, WIDTH), jnp.float32),
            jax.ShapeDtypeStruct((LEN, WIDTH), jnp.float32),
            jax.ShapeDtypeStruct((8, LEN), jnp.float32),
        ),
        in_specs=[ANY, ANY, VMEM, VMEM, VMEM],
        out_specs=(VMEM, VMEM, VMEM),
        scratch_shapes=[
            pltpu.VMEM((2, 8, 8, LEN), jnp.float32),
            pltpu.VMEM((4, 4, 2, 8, CAP, half), jnp.bfloat16),
            pltpu.VMEM((4, 8, LEN, half), jnp.bfloat16),
            pltpu.VMEM((4, 8, 2, CAP, half), jnp.bfloat16),
            pltpu.VMEM((4, 2, 2, HALF, half), jnp.bfloat16),
            pltpu.VMEM((4, 2, 2, LEN, half), jnp.bfloat16),
            pltpu.VMEM((4, LEN, half), jnp.bfloat16),
            pltpu.VMEM((2, 8, 8, LEN), jnp.float32),
            pltpu.VMEM((2, 7, 8, LEN), jnp.float32),
            pltpu.SemaphoreType.DMA((COLLECT_SEMS,)),
            pltpu.SemaphoreType.DMA((COLLECT_SEMS,)),
        ],
        compiler_params=params(4),
    )(results, back_results, table, gates, tokens)


def small_sum_kernel(part, total, got, send, recv):
    me = lax.axis_index("grp")
    links = Links(send, recv)
    peers = [(me + shift) % 8 for shift in range(1, 8)]
    ids = links.ids(7)
    greet("grp", peers)
    copies = [
        links.start(part, got.at[me], ids[i], "grp", peers[i]) for i in range(7)
    ]
    got[me] = part[...]
    for copy in copies:
        copy.wait_recv()
    summed = got[0]
    for i in range(1, 8):
        summed = summed + got[i]
    total[...] = summed
    links.finish()


def small_sum(part, collective_id, name):
    shape = part.shape
    return pl.pallas_call(
        small_sum_kernel,
        name=name,
        out_shape=jax.ShapeDtypeStruct(shape, jnp.float32),
        in_specs=[VMEM],
        out_specs=VMEM,
        scratch_shapes=[
            pltpu.VMEM((8,) + shape, jnp.float32),
            pltpu.SemaphoreType.DMA((7,)),
            pltpu.SemaphoreType.DMA((7,)),
        ],
        compiler_params=params(collective_id),
    )(part)


KEYS = 512


def attend_kernel(firsts, query, kv, first_key, query_pos, inputs, resid, best, total, acc):
    scale = HEAD_DIM ** (-0.5) * 1.4426950408889634
    groups = HEADS // KV_HEADS
    best[...] = jnp.full(best.shape, -1e30, jnp.float32)
    total[...] = jnp.zeros(total.shape, jnp.float32)
    acc[...] = jnp.zeros(acc.shape, jnp.float32)

    def step(masked, i, carry):
        start = pl.multiple_of(i * KEYS, KEYS)
        keys = kv[pl.ds(start, KEYS), pl.ds(0, HEAD_DIM)]
        values = kv[pl.ds(start, KEYS), pl.ds(HEAD_DIM, HEAD_DIM)]
        if masked:
            key_pos = start + lax.broadcasted_iota(jnp.int32, (LEN, KEYS), 1)
            allowed = (key_pos <= query_pos[...]) & (key_pos >= first_key[...])
        for h in range(groups):
            scores = lax.dot_general(
                query[:, h * HEAD_DIM : (h + 1) * HEAD_DIM],
                keys,
                (((1,), (1,)), ((), ())),
                preferred_element_type=jnp.float32,
            )
            if masked:
                scores = jnp.where(allowed, scores, -1e30)
            old = best[h]
            new = jnp.maximum(old, jnp.max(scores, axis=1, keepdims=True))
            weights = jnp.exp2((scores - new) * scale)
            shrink = jnp.exp2((old - new) * scale)
            best[h] = new
            total[h] = total[h] * shrink + jnp.sum(weights, axis=1, keepdims=True)
            acc[h] = acc[h] * shrink + jnp.dot(
                weights.astype(jnp.bfloat16), values, preferred_element_type=jnp.float32
            )
        return carry

    first_query = lax.axis_index("seq") * LEN
    low = firsts[0] // KEYS
    high = (first_query + LEN + KEYS - 1) // KEYS
    full_low = jnp.minimum((firsts[LEN - 1] + KEYS - 1) // KEYS, high)
    full_high = jnp.maximum((first_query + 1) // KEYS, full_low)
    lax.fori_loop(low, full_low, functools.partial(step, True), 0)
    lax.fori_loop(full_low, full_high, functools.partial(step, False), 0)
    lax.fori_loop(full_high, high, functools.partial(step, True), 0)
    for h in range(groups):
        cols = slice(h * HEAD_DIM, (h + 1) * HEAD_DIM)
        attended = (acc[h] / total[h]).astype(jnp.bfloat16).astype(jnp.float32)
        resid[:, cols] = (inputs[:, cols].astype(jnp.float32) + attended).astype(jnp.bfloat16)


def attend(query, kv, doc_ids, inputs):
    first_query = lax.axis_index("seq") * LEN
    query_pos = first_query + jnp.arange(LEN, dtype=jnp.int32)
    query_doc = lax.dynamic_slice_in_dim(doc_ids, first_query, LEN)
    firsts = jnp.sum((doc_ids[None, :] < query_doc[:, None]).astype(jnp.int32), axis=1)
    first_key = firsts[:, None]
    groups = HEADS // KV_HEADS
    return pl.pallas_call(
        attend_kernel,
        name="attend",
        out_shape=jax.ShapeDtypeStruct((LEN, WIDTH), jnp.bfloat16),
        in_specs=[pl.BlockSpec(memory_space=pltpu.SMEM)] + [VMEM] * 5,
        out_specs=VMEM,
        scratch_shapes=[
            pltpu.VMEM((groups, LEN, 1), jnp.float32),
            pltpu.VMEM((groups, LEN, 1), jnp.float32),
            pltpu.VMEM((groups, LEN, HEAD_DIM), jnp.float32),
        ],
        compiler_params=params(),
    )(firsts, query, kv, first_key, query_pos[:, None], inputs)


def product_kernel(turned, rows, weight, out):
    out[0] = lax.dot_general(
        rows[0],
        weight[0],
        (((1,), (1 if turned else 0,)), ((), ())),
        preferred_element_type=jnp.float32,
    ).astype(jnp.bfloat16)


def product(rows, weight, turned, name):
    sets, count, depth = rows.shape
    width = weight.shape[1 if turned else 2]
    return pl.pallas_call(
        functools.partial(product_kernel, turned),
        name=name,
        grid=(sets,),
        out_shape=jax.ShapeDtypeStruct((sets, count, width), jnp.bfloat16),
        in_specs=[
            pl.BlockSpec((1, count, depth), lambda m: (m, 0, 0)),
            pl.BlockSpec((1,) + weight.shape[1:], lambda m: (m, 0, 0)),
        ],
        out_specs=pl.BlockSpec((1, count, width), lambda m: (m, 0, 0)),
        compiler_params=params(),
        cost_estimate=pl.CostEstimate(
            flops=2 * sets * count * depth * width,
            bytes_accessed=2 * sets * (count * depth + depth * width + count * width),
            transcendentals=0,
        ),
    )(rows, weight)


def row_product_kernel(rows, gain, weight, out, squares):
    wide = rows[0].astype(jnp.float32)
    out[0] = jnp.dot(
        (wide * gain[...]).astype(jnp.bfloat16), weight[0], preferred_element_type=jnp.float32
    ).astype(jnp.bfloat16)
    squares[0] = lax.dot_general(
        jnp.ones((8, WIDTH), jnp.float32),
        wide * wide,
        (((1,), (1,)), ((), ())),
        precision=lax.Precision.HIGHEST,
        preferred_element_type=jnp.float32,
    )


def row_product(rows, gain, weight):
    sets, count, depth = rows.shape
    return pl.pallas_call(
        row_product_kernel,
        name="row_product",
        grid=(sets,),
        out_shape=(
            jax.ShapeDtypeStruct((sets, count, FF), jnp.bfloat16),
            jax.ShapeDtypeStruct((sets, 8, count), jnp.float32),
        ),
        in_specs=[
            pl.BlockSpec((1, count, depth), lambda m: (m, 0, 0)),
            pl.BlockSpec((1, depth), lambda m: (0, 0)),
            pl.BlockSpec((1,) + weight.shape[1:], lambda m: (m, 0, 0)),
        ],
        out_specs=(
            pl.BlockSpec((1, count, FF), lambda m: (m, 0, 0)),
            pl.BlockSpec((1, 8, count), lambda m: (m, 0, 0)),
        ),
        compiler_params=params(),
        cost_estimate=pl.CostEstimate(
            flops=2 * sets * count * depth * FF,
            bytes_accessed=2 * sets * (count * depth + depth * FF + count * FF),
            transcendentals=0,
        ),
    )(rows, gain[None, :], weight)


def expert_kernel(pre, inverse, act_grad, w_out, w_in, out, grad):
    root = 0.7978845608028654
    wide = pre[0].astype(jnp.float32) * inverse[0]
    square = wide * wide
    curve = jnp.tanh(root * wide * (1.0 + 0.044715 * square))
    active = (0.5 * wide * (1.0 + curve)).astype(jnp.bfloat16)
    out[0] = jnp.dot(active, w_out[0], preferred_element_type=jnp.float32).astype(jnp.bfloat16)
    slope = 0.5 * (1.0 + curve) + (0.5 * root) * wide * (1.0 - curve * curve) * (
        1.0 + 3 * 0.044715 * square
    )
    pre_grad = (slope * act_grad[0].astype(jnp.float32)).astype(jnp.bfloat16)
    grad[0] = lax.dot_general(
        pre_grad, w_in[0], (((1,), (1,)), ((), ())), preferred_element_type=jnp.float32
    ).astype(jnp.bfloat16)


def expert_products(pre, inverse, act_grad, w_out, w_in):
    sets, count, _ = pre.shape
    tile = 256

    def moving(width):
        return pl.BlockSpec((1, tile, width), lambda m, i: (m, i, 0))

    def held(weight):
        return pl.BlockSpec((1,) + weight.shape[1:], lambda m, i: (m, 0, 0))

    shape = jax.ShapeDtypeStruct((sets, count, WIDTH), jnp.bfloat16)
    return pl.pallas_call(
        expert_kernel,
        name="expert_products",
        grid=(sets, count // tile),
        out_shape=(shape, shape),
        in_specs=[moving(FF), moving(1), moving(FF), held(w_out), held(w_in)],
        out_specs=(moving(WIDTH), moving(WIDTH)),
        compiler_params=params(),
        cost_estimate=pl.CostEstimate(
            flops=4 * sets * count * FF * WIDTH,
            bytes_accessed=4 * sets * (count * (FF + WIDTH) + FF * WIDTH),
            transcendentals=sets * count * FF,
        ),
    )(pre, inverse, act_grad, w_out, w_in)


def body(
    inputs,
    query_states,
    key_states,
    value_states,
    doc_ids,
    modality,
    expert_ids,
    norm_gain,
    router_w,
    w_in,
    w_out,
    grad_out,
):
    length, width = inputs.shape
    experts = lax.axis_size("seq")
    kept_mask = expert_ids >= 0
    kept_wide = kept_mask.astype(jnp.float32)
    column = modality[:, None] * experts + jnp.where(kept_mask, expert_ids, 0)
    one_hot = (
        column[:, :, None] == jnp.arange(2 * experts, dtype=jnp.int32)[None, None, :]
    ) & kept_mask[:, :, None]
    entries = length * TOP
    flat_hot = one_hot.reshape(entries, 2 * experts).astype(jnp.bfloat16)
    entry_range = jnp.arange(entries, dtype=jnp.int32)
    earlier = (entry_range[:, None] > entry_range[None, :]).astype(jnp.bfloat16)
    before = jnp.dot(earlier, flat_hot, preferred_element_type=jnp.float32)
    slot_rank = jnp.sum(before * flat_hot.astype(jnp.float32), axis=1).astype(jnp.int32)
    slots = jnp.where(kept_mask, column * CAP + slot_rank.reshape(length, TOP), -1)
    slots = jnp.concatenate([slots.T, jnp.full((8 - TOP, length), -1, jnp.int32)], axis=0)

    w_in_local = w_in[:, 0]
    w_out_local = w_out[:, 0]

    got_grads, tokens_grad, table, kv = dispatch_first(
        grad_out, slots, jnp.concatenate([key_states, value_states], axis=1)
    )
    entries_all = experts * CAP
    back_part = product(
        got_grads.reshape(2, entries_all, width), w_out_local, True, "back_product"
    )
    resid_state = attend(query_states, kv.reshape(experts * length, 2 * HEAD_DIM), doc_ids, inputs)
    state_wide = resid_state.astype(jnp.float32)
    scaled = state_wide * norm_gain[None, :]
    raw_part = lax.dot_general(
        router_w,
        scaled.astype(jnp.bfloat16),
        (((0,), (1,)), ((), ())),
        preferred_element_type=jnp.float32,
    )
    square_part = jnp.sum(state_wide * state_wide, axis=1)[None, :]
    got_rows, stats, act_grad = dispatch_rows(
        resid_state,
        table,
        jnp.concatenate([raw_part, square_part, jnp.zeros((7, length), jnp.float32)], axis=0),
        back_part.reshape(2 * entries_all, FF),
    )
    inv_row = lax.rsqrt(stats[2 * experts] / D + eps_norm)
    inv_rms = inv_row[:, None]
    raw_logits = stats[: 2 * experts].T
    logits = raw_logits * inv_rms
    chosen = jnp.sum(jnp.where(one_hot, logits[:, None, :], 0.0), axis=2)
    lifted = jax.nn.sigmoid(chosen)
    denominator = gate_offset + jnp.sum(kept_wide * lifted, axis=1, keepdims=True)
    gates = kept_wide * lifted / denominator
    gates_t = jnp.concatenate([gates.T, jnp.zeros((8 - TOP, length), jnp.float32)], axis=0)

    row_part, squares = row_product(
        got_rows.reshape(2, entries_all, width), norm_gain, w_in_local
    )
    pre_act, square_sum = line_sum(
        row_part.reshape(2 * entries_all, FF), squares[:, 0].reshape(8, LEN)
    )
    pre_act = pre_act.reshape(2, entries_all, FF)
    inverse = lax.rsqrt(square_sum / D + eps_norm).reshape(2, entries_all, 1)
    expert_out, entry_grad = expert_products(
        pre_act, inverse, act_grad.reshape(2, entries_all, FF), w_out_local, w_in_local
    )
    mixture, entry_sum, gate_part = collect(
        expert_out.reshape(2, experts, CAP, width),
        entry_grad.reshape(2, experts, CAP, width),
        table,
        gates_t,
        tokens_grad,
    )
    layer_out = (state_wide + mixture).astype(jnp.bfloat16)
    entry_dot = jnp.sum(entry_sum * scaled, axis=1)[None, :]
    row_index = jnp.arange(8, dtype=jnp.int32)[:, None]
    ends = small_sum(jnp.where(row_index == TOP, entry_dot, gate_part), 7, "sum_ends")
    gate_grad = ends[:TOP].T
    gate_dot = jnp.sum(gates * gate_grad, axis=1, keepdims=True)
    logit_grad = kept_wide * (gate_grad - gate_dot) / denominator * lifted * (1.0 - lifted)
    logit_full = jnp.sum(jnp.where(one_hot, logit_grad[:, :, None], 0.0), axis=1)
    router_grad = jnp.dot(
        logit_full, router_w.astype(jnp.float32).T, precision=lax.Precision.HIGHEST
    )
    norm_dot = ends[TOP][:, None] + jnp.sum(logit_full * raw_logits, axis=1, keepdims=True)
    normed_grad = router_grad + entry_sum
    state_grad = (
        grad_out.astype(jnp.float32)
        + inv_rms * norm_gain[None, :] * normed_grad
        - inv_rms**3 / D * state_wide * norm_dot
    )
    return (layer_out, state_grad.astype(jnp.bfloat16))


def solution(mesh):
    in_specs = (
        P("seq", "grp"),
        P("seq", "grp"),
        P("seq", "grp"),
        P("seq", "grp"),
        P(),
        P("seq"),
        P("seq", None),
        P("grp"),
        P("grp", None),
        P(None, "seq", "grp", None),
        P(None, "seq", None, "grp"),
        P("seq", "grp"),
    )
    out_specs = (P("seq", "grp"), P("seq", "grp"))
    return jax.shard_map(body, mesh=mesh, in_specs=in_specs, out_specs=out_specs, check_vma=False)
```
